128 devices in a mesh: chan: 8 (over x, z_hi), space: 16 (over z_lo, y, core).
Axes of the slice: x: 4, y: 4, z: 4 (z_hi: 2, z_lo: 2; z = z_hi * 2 + z_lo), core: 2. Of those that a mesh axis runs over, the one named last changes fastest.
Arguments:
- volume: bfloat16 [128, 128, 8, 256], P(None, 'space', None, 'chan'), may hold values from -6 to 6
- first_filters: bfloat16 [3, 3, 3, 256, 256], P(None, None, None, None, 'chan'), may hold values from -0.078125 to 0.078125
- second_filters: bfloat16 [3, 3, 3, 256, 256], replicated, may hold values from -0.078125 to 0.078125
- out_grad: bfloat16 [128, 128, 8, 256], P('chan', 'space'), may hold values from -6 to 6
Outputs:
- act_grad: bfloat16 [128, 128, 8, 256], P('chan', 'space')
- filter_grad: float32 [3, 3, 3, 256, 256], replicated
The draws below stay inside these ranges and needn't reach their ends.
All inputs are finite; a program needn't handle non-finite values.
Results may differ from the reference program's by a relative error of at most 0.0055.
Values may be sent and summed in bfloat16 or wider, within the bound.
No kernel may reach another device: no remote copies, remote signals or barrier semaphores. Data moves between devices by JAX's collectives and lax.ppermute only.
A program may use at most 128 MiB of HBM per device.

```python
import math
import jax
import jax.numpy as jnp
from jax import lax

CH = 256
NZ = 8
NX = 128
NY = 128


def block_scale(key, shape, pieces, low, high):
    loudness, own = 1.0, jax.random.fold_in(key, 6)
    for axis_at, blocks in pieces:
        draws = jnp.exp(jax.random.uniform(jax.random.fold_in(own, axis_at), (blocks,), jnp.float32, low / len(pieces), high / len(pieces)))
        loudness = loudness * jnp.repeat(draws, shape[axis_at] // blocks).reshape([-1 if axis == axis_at else 1 for axis in range(len(shape))])
    return loudness


def gaussian(rng, extent, width, most, cuts=(), kind=jnp.bfloat16):
    values = jax.random.normal(rng, extent, jnp.float32) * width
    if len(cuts) > 0:
        values = block_scale(rng, extent, cuts, -0.22, 0.18) * values
    return jnp.clip(values, min=-most, max=most).astype(kind)


def setup_inputs(seed: int = 0) -> dict:
    streams_of = jax.random.split(jax.random.key(seed), 5)
    volume = gaussian(streams_of[0], (NX, NY, NZ, CH), 1.0, 6.0, ((1, 16), (3, 8)))
    first_filters = gaussian(streams_of[1], (3, 3, 3, CH, CH), (27 * CH) ** -0.5, 0.078125, ((4, 8),))
    second_filters = gaussian(streams_of[2], (3, 3, 3, CH, CH), (27 * CH) ** -0.5, 0.078125)
    out_grad = gaussian(streams_of[3], (NX, NY, NZ, CH), 1.0, 6.0, ((0, 8), (1, 16)))
    return dict(volume=volume, first_filters=first_filters, second_filters=second_filters, out_grad=out_grad)


def pad_cells(field):
    return jnp.pad(field, ((1, 1), (1, 1), (1, 1), (0, 0)))

def conv_valid(padded, kernel):
    return lax.conv_general_dilated(padded[None].astype(jnp.float32), kernel.astype(jnp.float32), (1, 1, 1), 'VALID', dimension_numbers=('NDHWC', 'DHWIO', 'NDHWC'), precision=lax.Precision.HIGHEST)[0]

def reference(volume, first_filters, second_filters, out_grad):
    first_pre = conv_valid(pad_cells(volume), first_filters)
    activation = jax.nn.silu(first_pre).astype(jnp.bfloat16)
    padded_act = pad_cells(activation)
    second_pre = conv_valid(padded_act, second_filters)
    sigmoid_h = jax.nn.sigmoid(second_pre)
    delta_out = (out_grad.astype(jnp.float32) * sigmoid_h * (1.0 + second_pre * (1.0 - sigmoid_h))).astype(jnp.bfloat16)
    swapped = jnp.swapaxes(second_filters[::-1, ::-1, ::-1], 3, 4)
    act_grad = conv_valid(pad_cells(delta_out), swapped).astype(jnp.bfloat16)
    flat_delta = delta_out.reshape(-1, CH)
    rows_out = []
    for shift_x in range(3):
        for shift_y in range(3):
            for shift_z in range(3):
                window = padded_act[shift_x:shift_x + NX, shift_y:shift_y + NY, shift_z:shift_z + NZ]
                rows_out.append(lax.dot_general(window.reshape(-1, CH), flat_delta, (((0,), (0,)), ((), ())), preferred_element_type=jnp.float32))
    filter_grad = jnp.stack(rows_out).reshape(3, 3, 3, CH, CH) * (1.0 / math.sqrt(NX * NY * NZ))
    return (act_grad, filter_grad)
```

```python
import math

import jax
import jax.numpy as jnp
import numpy as np
from jax import lax
from jax.experimental import pallas as pl
from jax.experimental.pallas import tpu as pltpu
from jax.sharding import Mesh
from jax.sharding import PartitionSpec as P

BF = jnp.bfloat16
F32 = jnp.float32
C = 256
NZ = 8
BX, BY = 16, 8
HALF = 3456
SLOT = 3584
CHIPS = ("chan", "slab")
VMEM = pl.BlockSpec(memory_space=pltpu.VMEM)
SMEM = pl.BlockSpec(memory_space=pltpu.SMEM)


def params(limit=60 << 20):
    return pltpu.CompilerParams(vmem_limit_bytes=limit)


def cost(flops, moved):
    return pl.CostEstimate(flops=int(flops), bytes_accessed=int(moved), transcendentals=0)


def dot_t(a, b):
    return lax.dot_general(a, b, (((1,), (1,)), ((), ())), preferred_element_type=F32)


def dot_n(a, b):
    return lax.dot_general(a, b, (((1,), (0,)), ((), ())), preferred_element_type=F32)


def pack_kernel(pick_ref, vol_ref, out_ref, wide_ref):
    pick = pick_ref[...]
    for quad in range(2):
        for z in range(NZ):
            rows = jnp.concatenate([vol_ref[quad * 4 + j, z] for j in range(4)], axis=0)
            wide_ref[pl.ds(quad * 8 + z, 176, stride=16), :] = dot_t(pick, rows)
    out_ref[...] = wide_ref[...].astype(BF)


def neighbours(value):
    z = lax.broadcasted_iota(jnp.int32, value.shape, 1)
    before = jnp.where(z == 0, 0.0, pltpu.roll(value, 1, 1))
    after = jnp.where(z == NZ - 1, 0.0, pltpu.roll(value, NZ - 1, 1))
    return before.astype(BF), after.astype(BF)


def layers_kernel(
    place_ref, near_ref, low_ref, high_ref, mine_ref, other_ref, w2_ref,
    grad_ref, gxl_ref, gxh_ref, gyl_ref, gyh_ref,
    keep_ref, send_ref, d3_ref,
    v3_ref, a3_ref, w1_ref, acc_ref, og_ref, dt_ref, g_ref,
):
    chan, space, core = place_ref[0], place_ref[1], place_ref[2]

    def place_filters(d, carry):
        owner = lax.rem(chan - d + 8, 8)
        for stack, half in ((mine_ref, core), (other_ref, 1 - core)):
            at = pl.multiple_of(owner * 32 + half * 16, 16)
            for t in range(27):
                w1_ref[t // 3, pl.ds(at, 16), (t % 3) * C : (t % 3 + 1) * C] = stack[d, t]
        return carry

    lax.fori_loop(0, 8, place_filters, 0)

    row = lax.broadcasted_iota(jnp.int32, (1024, C), 0)
    col = lax.broadcasted_iota(jnp.int32, (1024, C), 1)
    same = ((row >> 7) == (col >> 5)) & ((row & 31) == (col & 31))
    for j in range(4):
        sel = (same & (((row >> 5) & 3) == j)).astype(F32).astype(BF)
        for b in range(4):
            y = b * 4 + j - 1
            if y < 0 or y >= 14:
                continue
            src = (low_ref, near_ref, near_ref, high_ref)[b]
            at = 8 if b == 2 else 0
            rows = jnp.concatenate(
                [src[c, :, at : at + 8, :].reshape(176, 128) for c in range(8)], axis=1
            )
            value = dot_n(rows, sel).reshape(22, NZ, C)
            before, after = neighbours(value)
            v3_ref[:, y * 8 : y * 8 + 8, 0:C] = before
            v3_ref[:, y * 8 : y * 8 + 8, C : 2 * C] = value.astype(BF)
            v3_ref[:, y * 8 : y * 8 + 8, 2 * C : 3 * C] = after

    def first(i, carry):
        x0 = i * 5
        for s in range(9):
            part = v3_ref[pl.ds(x0 + s // 3, 5), (s % 3) * 8 : (s % 3) * 8 + 96, :]
            part = dot_t(part.reshape(480, 3 * C), w1_ref[s])
            if s == 0:
                acc_ref[...] = part
            else:
                acc_ref[...] += part
        v = acc_ref[...]
        act = (v / (1.0 + jnp.exp(-v))).astype(BF)
        wide = act.astype(F32).reshape(60, NZ, C)
        before, after = neighbours(wide)
        a3_ref[pl.ds(x0, 5), :, 0:C] = before.reshape(5, 96, C)
        a3_ref[pl.ds(x0, 5), :, C : 2 * C] = act.reshape(5, 96, C)
        a3_ref[pl.ds(x0, 5), :, 2 * C : 3 * C] = after.reshape(5, 96, C)
        return carry

    lax.fori_loop(0, 4, first, 0)

    @pl.when(chan == 0)
    def _():
        a3_ref[0:2] = jnp.zeros((2, 96, 3 * C), BF)

    @pl.when(chan == 7)
    def _():
        a3_ref[18:20] = jnp.zeros((2, 96, 3 * C), BF)

    @pl.when(space == 0)
    def _():
        a3_ref[:, 0:16, :] = jnp.zeros((20, 16, 3 * C), BF)

    @pl.when(space == 15)
    def _():
        a3_ref[:, 80:96, :] = jnp.zeros((20, 16, 3 * C), BF)

    og_ref[1:17, 8:72, :] = grad_ref[...]
    og_ref[0:1, 8:72, :] = gxl_ref[...]
    og_ref[17:18, 8:72, :] = gxh_ref[...]
    og_ref[:, 0:8, :] = gyl_ref[...]
    og_ref[:, 72:80, :] = gyh_ref[...]

    def second(i, carry):
        x0 = i * 6
        for s in range(9):
            part = a3_ref[pl.ds(x0 + s // 3, 6), (s % 3) * 8 : (s % 3) * 8 + 80, :]
            part = dot_n(part.reshape(480, 3 * C), w2_ref[s])
            if s == 0:
                acc_ref[...] = part
            else:
                acc_ref[...] += part
        v = acc_ref[...]
        sig = 1.0 / (1.0 + jnp.exp(-v))
        og = og_ref[pl.ds(x0, 6)].reshape(480, C).astype(F32)
        delta = (og * sig * (1.0 + v * (1.0 - sig))).astype(BF)
        before, after = neighbours(delta.astype(F32).reshape(60, NZ, C))
        d3_ref[pl.ds(x0, 6), :, 0:C] = after.reshape(6, 80, C)
        d3_ref[pl.ds(x0, 6), :, C : 2 * C] = delta.reshape(6, 80, C)
        d3_ref[pl.ds(x0, 6), :, 2 * C : 3 * C] = before.reshape(6, 80, C)
        return carry

    lax.fori_loop(0, 3, second, 0)

    dt_ref[...] = d3_ref[1:17, 8:72, C : 2 * C].reshape(1024, C).T
    for s in range(9):
        part = a3_ref[1 + s // 3 : 17 + s // 3, (1 + s % 3) * 8 : (1 + s % 3) * 8 + 64, :]
        g = dot_n(dt_ref[...], part.reshape(1024, 3 * C)).astype(BF)
        for tz in range(3):
            t = 3 * s + tz
            tile = g[:, tz * C : (tz + 1) * C]
            for h in range(2):
                at = t * C + h * 128
                at += SLOT - HALF if at >= HALF else 0
                g_ref[at : at + 128, :] = tile[h * 128 : h * 128 + 128]
    zero = jnp.zeros((SLOT - HALF, C), BF)
    g_ref[HALF:SLOT, :] = zero
    g_ref[SLOT + HALF : 2 * SLOT, :] = zero
    keep_ref[...] = g_ref[pl.ds(pl.multiple_of(core * SLOT, 16), SLOT), :]
    send_ref[...] = g_ref[pl.ds(pl.multiple_of((1 - core) * SLOT, 16), SLOT), :]


def back_kernel(d3_ref, w2_ref, out_ref, acc_ref):
    def block(i, carry):
        x0 = i * 8
        for s in range(9):
            tx, ty = s // 3, s % 3
            part = d3_ref[pl.ds(x0 + 2 - tx, 8), (2 - ty) * 8 : (2 - ty) * 8 + 64, :]
            w = jnp.concatenate([w2_ref[s, k * C : (k + 1) * C, :] for k in range(3)], axis=1)
            part = dot_t(part.reshape(512, 3 * C), w)
            if s == 0:
                acc_ref[...] = part
            else:
                acc_ref[...] += part
        out_ref[pl.ds(x0, 8)] = acc_ref[...].astype(BF).reshape(8, 64, C)
        return carry

    lax.fori_loop(0, 2, block, 0)


def finish_kernel(place_ref, mine_ref, other_ref, out_ref, full_ref):
    core = place_ref[2]

    @pl.when(pl.program_id(0) == 0)
    def _():
        at = pl.multiple_of(core * HALF, 16)
        full_ref[pl.ds(at, HALF), :] = mine_ref[0:HALF, :]
        at = pl.multiple_of((1 - core) * HALF, 16)
        full_ref[pl.ds(at, HALF), :] = other_ref[0:HALF, :]

    row = lax.broadcasted_iota(jnp.int32, (C, C), 0)
    col = lax.broadcasted_iota(jnp.int32, (C, C), 1)
    unit = (row == col).astype(F32).astype(BF)
    at = pl.multiple_of(pl.program_id(0) * C, C)
    out_ref[0] = dot_t(unit, full_ref[pl.ds(at, C), :])


def border(count):
    up = [(i, i + 1) for i in range(count - 1)]
    return up, [(b, a) for a, b in up]


def local(volume, first_filters, second_filters, out_grad):
    chan, slab, core = (lax.axis_index(a) for a in ("chan", "slab", "core"))
    place = jnp.stack([chan, slab * 2 + core, core]).astype(jnp.int32)
    swap = [(0, 1), (1, 0)]
    up, down = border(16)
    xup, xdown = border(8)
    space = ("slab", "core")

    w1 = jnp.transpose(first_filters, (0, 1, 2, 4, 3)).reshape(27, 32, C)
    half = lax.dynamic_slice_in_dim(w1, core * 16, 16, axis=1)
    pieces = [half] + [
        lax.ppermute(half, "chan", [(i, (i + d) % 8) for i in range(8)]) for d in range(1, 8)
    ]

    og = out_grad.reshape(BX, BY * NZ, C)
    gxl = lax.ppermute(og[BX - 1 :], "chan", xup)
    gxh = lax.ppermute(og[:1], "chan", xdown)
    top = jnp.concatenate([gxl[:, 56:], og[:, 56:], gxh[:, 56:]], axis=0)
    bottom = jnp.concatenate([gxl[:, :8], og[:, :8], gxh[:, :8]], axis=0)
    gyl = lax.ppermute(top, space, up)
    gyh = lax.ppermute(bottom, space, down)

    pick = np.zeros((176, 128), np.float32)
    for c in range(8):
        for j in range(22):
            if 0 <= 16 * c - 3 + j < 128:
                pick[c * 22 + j, 16 * c - 3 + j] = 1.0
    packed = pl.pallas_call(
        pack_kernel,
        out_shape=jax.ShapeDtypeStruct((176 * 16, 128), BF),
        in_specs=[VMEM, VMEM],
        out_specs=VMEM,
        scratch_shapes=[pltpu.VMEM((176 * 16, 128), F32)],
        compiler_params=params(),
        cost_estimate=cost(16 * 176 * 128 * 256, 3 << 20),
        name="pack",
    )(jnp.asarray(pick, BF), jnp.transpose(volume, (1, 2, 3, 0)))
    near = lax.all_to_all(packed.reshape(8, 352, 128), "chan", 0, 0, tiled=True)
    near = near.reshape(8, 22, 16, 128)
    low = lax.ppermute(near[:, :, 8:], space, up)
    high = lax.ppermute(near[:, :, :8], space, down)

    mine = jnp.stack(pieces)
    other = lax.ppermute(mine, "core", swap)

    w2 = second_filters.reshape(9, 3 * C, C)
    keep, send, d3 = pl.pallas_call(
        layers_kernel,
        out_shape=(
            jax.ShapeDtypeStruct((SLOT, C), BF),
            jax.ShapeDtypeStruct((SLOT, C), BF),
            jax.ShapeDtypeStruct((18, 80, 3 * C), BF),
        ),
        in_specs=[SMEM] + [VMEM] * 11,
        out_specs=(VMEM, VMEM, VMEM),
        scratch_shapes=[
            pltpu.VMEM((22, 112, 3 * C), BF),
            pltpu.VMEM((20, 96, 3 * C), BF),
            pltpu.VMEM((9, C, 3 * C), BF),
            pltpu.VMEM((480, C), F32),
            pltpu.VMEM((18, 80, C), BF),
            pltpu.VMEM((C, 1024), BF),
            pltpu.VMEM((2 * SLOT, C), BF),
        ],
        compiler_params=params(),
        cost_estimate=cost(16e9, 20 << 20),
        name="layers",
    )(place, near, low, high, mine, other, w2, og, gxl, gxh, gyl, gyh)

    received = lax.ppermute(send, "core", swap)
    act_grad = pl.pallas_call(
        back_kernel,
        out_shape=jax.ShapeDtypeStruct((BX, BY * NZ, C), BF),
        in_specs=[VMEM, VMEM],
        out_specs=VMEM,
        scratch_shapes=[pltpu.VMEM((512, C), F32)],
        compiler_params=params(),
        cost_estimate=cost(3.6e9, 7 << 20),
        name="back",
    )(d3, w2)

    both = (keep.astype(F32) + received.astype(F32)).astype(BF).reshape(64, 56, C)
    shares = lax.all_to_all(both, CHIPS, 0, 0, tiled=True)
    scale = 1.0 / math.sqrt(128 * 128 * NZ)
    share = (jnp.sum(shares.astype(F32), axis=0) * scale).astype(BF)
    spread = lax.optimization_barrier(jnp.broadcast_to(share[None], (64, 56, C)))
    ours = lax.all_to_all(spread, CHIPS, 0, 0, tiled=True).reshape(SLOT, C)
    theirs = lax.ppermute(ours, "core", swap)
    whole = pl.BlockSpec((SLOT, C), lambda t: (0, 0))
    filter_grad = pl.pallas_call(
        finish_kernel,
        grid=(27,),
        out_shape=jax.ShapeDtypeStruct((27, C, C), F32),
        in_specs=[SMEM, whole, whole],
        out_specs=pl.BlockSpec((1, C, C), lambda t: (t, 0, 0)),
        scratch_shapes=[pltpu.VMEM((2 * HALF, C), BF)],
        compiler_params=params(),
        cost_estimate=cost(1e9, 11 << 20),
        name="finish",
    )(place, ours, theirs)
    return (
        act_grad.reshape(BX, BY, NZ, C),
        filter_grad.reshape(3, 3, 3, C, C),
    )


def solution(mesh):
    cells = Mesh(mesh.devices.reshape(8, 8, 2), ("chan", "slab", "core"))
    space = ("slab", "core")
    placed = (
        P(None, space, None, "chan"),
        P(None, None, None, None, "chan"),
        P(),
        P("chan", space, None, None),
    )
    return jax.shard_map(
        local,
        mesh=cells,
        in_specs=placed,
        out_specs=(P("chan", space, None, None), P()),
        check_vma=False,
    )
```

```python
import math

import jax
import jax.numpy as jnp
import numpy as np
from jax import lax
from jax.experimental import pallas as pl
from jax.experimental.pallas import tpu as pltpu
from jax.sharding import Mesh
from jax.sharding import PartitionSpec as P

BF = jnp.bfloat16
F32 = jnp.float32
C = 256
NZ = 8
BX, BY = 16, 8
HALF = 3456
SLOT = 3584
CHIPS = ("chan", "slab")
VMEM = pl.BlockSpec(memory_space=pltpu.VMEM)
SMEM = pl.BlockSpec(memory_space=pltpu.SMEM)


def params(mib):
    return pltpu.CompilerParams(vmem_limit_bytes=mib << 20)


def cost(flops, moved):
    return pl.CostEstimate(flops=int(flops), bytes_accessed=int(moved), transcendentals=0)


def dot_t(a, b):
    return lax.dot_general(a, b, (((1,), (1,)), ((), ())), preferred_element_type=F32)


def dot_n(a, b):
    return lax.dot_general(a, b, (((1,), (0,)), ((), ())), preferred_element_type=F32)


def pack_kernel(pick_ref, vol_ref, out_ref, wide_ref):
    pick = pick_ref[...]
    for quad in range(2):
        for z in range(NZ):
            rows = jnp.concatenate([vol_ref[quad * 4 + j, z] for j in range(4)], axis=0)
            wide_ref[pl.ds(quad * 8 + z, 176, stride=16), :] = dot_t(pick, rows)
    out_ref[...] = wide_ref[...].astype(BF)


def neighbours(value):
    z = lax.broadcasted_iota(jnp.int32, value.shape, 1)
    before = jnp.where(z == 0, 0.0, pltpu.roll(value, 1, 1))
    after = jnp.where(z == NZ - 1, 0.0, pltpu.roll(value, NZ - 1, 1))
    return before.astype(BF), after.astype(BF)


def unpack_kernel(place_ref, near_ref, low_ref, high_ref, v3_ref):
    core = place_ref[2]
    row = lax.broadcasted_iota(jnp.int32, (1024, C), 0)
    col = lax.broadcasted_iota(jnp.int32, (1024, C), 1) ^ (core * 128)
    same = ((row >> 7) == (col >> 5)) & ((row & 31) == (col & 31))
    for j in range(4):
        sel = (same & (((row >> 5) & 3) == j)).astype(F32).astype(BF)
        for b in range(4):
            y = b * 4 + j - 1
            if y < 0 or y >= 14:
                continue
            src = (low_ref, near_ref, near_ref, high_ref)[b]
            at = 8 if b == 2 else 0
            rows = jnp.concatenate(
                [src[c, :, at : at + 8, :].reshape(176, 128) for c in range(8)], axis=1
            )
            value = dot_n(rows, sel).reshape(22, NZ, C)
            before, after = neighbours(value)
            v3_ref[:, y * 8 : y * 8 + 8, 0:C] = before
            v3_ref[:, y * 8 : y * 8 + 8, C : 2 * C] = value.astype(BF)
            v3_ref[:, y * 8 : y * 8 + 8, 2 * C : 3 * C] = after


def turn_kernel(pieces_ref, out_ref):
    def turn(s, carry):
        for k in range(3):
            rows = jnp.concatenate([pieces_ref[c, 3 * s + k] for c in range(8)], axis=0)
            out_ref[3 * s + k] = rows.T
        return carry

    lax.fori_loop(0, 9, turn, 0)


def layers_kernel(
    place_ref, v3_ref, mine_ref, other_ref, w2_ref,
    grad_ref, gxl_ref, gxh_ref, gyl_ref, gyh_ref,
    keep_ref, send_ref, d3_ref,
    a3_ref, acc_ref, og_ref, dt_ref, g_ref,
):
    chan, space, core = place_ref[0], place_ref[1], place_ref[2]

    def first(i, carry):
        x0 = i * 5
        for s in range(9):
            part = v3_ref[pl.ds(x0 + s // 3, 5), (s % 3) * 8 : (s % 3) * 8 + 96, :]
            w = [h[3 * s + k] for k in range(3) for h in (mine_ref, other_ref)]
            part = dot_n(part.reshape(480, 3 * C), jnp.concatenate(w, axis=0))
            if s == 0:
                acc_ref[...] = part
            else:
                acc_ref[...] += part
        v = acc_ref[...]
        act = (v / (1.0 + jnp.exp(-v))).astype(BF)
        wide = act.astype(F32).reshape(60, NZ, C)
        before, after = neighbours(wide)
        a3_ref[pl.ds(x0, 5), :, 0:C] = before.reshape(5, 96, C)
        a3_ref[pl.ds(x0, 5), :, C : 2 * C] = act.reshape(5, 96, C)
        a3_ref[pl.ds(x0, 5), :, 2 * C : 3 * C] = after.reshape(5, 96, C)
        return carry

    lax.fori_loop(0, 4, first, 0)

    @pl.when(chan == 0)
    def _():
        a3_ref[0:2] = jnp.zeros((2, 96, 3 * C), BF)

    @pl.when(chan == 7)
    def _():
        a3_ref[18:20] = jnp.zeros((2, 96, 3 * C), BF)

    @pl.when(space == 0)
    def _():
        a3_ref[:, 0:16, :] = jnp.zeros((20, 16, 3 * C), BF)

    @pl.when(space == 15)
    def _():
        a3_ref[:, 80:96, :] = jnp.zeros((20, 16, 3 * C), BF)

    og_ref[1:17, 8:72, :] = grad_ref[...]
    og_ref[0:1, 8:72, :] = gxl_ref[...]
    og_ref[17:18, 8:72, :] = gxh_ref[...]
    og_ref[:, 0:8, :] = gyl_ref[...]
    og_ref[:, 72:80, :] = gyh_ref[...]

    def second(i, carry):
        x0 = i * 6
        for s in range(9):
            part = a3_ref[pl.ds(x0 + s // 3, 6), (s % 3) * 8 : (s % 3) * 8 + 80, :]
            part = dot_n(part.reshape(480, 3 * C), w2_ref[s])
            if s == 0:
                acc_ref[...] = part
            else:
                acc_ref[...] += part
        v = acc_ref[...]
        sig = 1.0 / (1.0 + jnp.exp(-v))
        og = og_ref[pl.ds(x0, 6)].reshape(480, C).astype(F32)
        delta = (og * sig * (1.0 + v * (1.0 - sig))).astype(BF)
        before, after = neighbours(delta.astype(F32).reshape(60, NZ, C))
        d3_ref[pl.ds(x0, 6), :, 0:C] = after.reshape(6, 80, C)
        d3_ref[pl.ds(x0, 6), :, C : 2 * C] = delta.reshape(6, 80, C)
        d3_ref[pl.ds(x0, 6), :, 2 * C : 3 * C] = before.reshape(6, 80, C)
        return carry

    lax.fori_loop(0, 3, second, 0)

    dt_ref[...] = d3_ref[1:17, 8:72, C : 2 * C].reshape(1024, C).T
    for s in range(9):
        part = a3_ref[1 + s // 3 : 17 + s // 3, (1 + s % 3) * 8 : (1 + s % 3) * 8 + 64, :]
        g = dot_n(dt_ref[...], part.reshape(1024, 3 * C)).astype(BF)
        for tz in range(3):
            t = 3 * s + tz
            tile = g[:, tz * C : (tz + 1) * C]
            for h in range(2):
                at = t * C + h * 128
                at += SLOT - HALF if at >= HALF else 0
                g_ref[at : at + 128, :] = tile[h * 128 : h * 128 + 128]
    zero = jnp.zeros((SLOT - HALF, C), BF)
    g_ref[HALF:SLOT, :] = zero
    g_ref[SLOT + HALF : 2 * SLOT, :] = zero
    keep_ref[...] = g_ref[pl.ds(pl.multiple_of(core * SLOT, 16), SLOT), :]
    send_ref[...] = g_ref[pl.ds(pl.multiple_of((1 - core) * SLOT, 16), SLOT), :]


def flip_kernel(w_ref, out_ref):
    def turn(s, carry):
        for k in range(3):
            out_ref[s, k * C : (k + 1) * C, :] = w_ref[s, k * C : (k + 1) * C, :].T
        return carry

    lax.fori_loop(0, 9, turn, 0)


def back_kernel(d3_ref, w2_ref, out_ref, acc_ref):
    for s in range(9):
        tx, ty = s // 3, s % 3
        part = d3_ref[2 - tx : 18 - tx, (2 - ty) * 8 : (2 - ty) * 8 + 64, :]
        part = dot_n(part.reshape(1024, 3 * C), w2_ref[s])
        if s == 0:
            acc_ref[...] = part
        elif s < 8:
            acc_ref[...] += part
        else:
            out_ref[...] = (acc_ref[...] + part).astype(BF).reshape(BX, 64, C)


def finish_kernel(place_ref, mine_ref, other_ref, out_ref, full_ref):
    core = place_ref[2]

    @pl.when(pl.program_id(0) == 0)
    def _():
        at = pl.multiple_of(core * HALF, 16)
        full_ref[pl.ds(at, HALF), :] = mine_ref[0:HALF, :]
        at = pl.multiple_of((1 - core) * HALF, 16)
        full_ref[pl.ds(at, HALF), :] = other_ref[0:HALF, :]

    row = lax.broadcasted_iota(jnp.int32, (C, C), 0)
    col = lax.broadcasted_iota(jnp.int32, (C, C), 1)
    unit = (row == col).astype(F32).astype(BF)
    for k in range(3):
        at = pl.multiple_of(pl.program_id(0) * 3 * C + k * C, C)
        out_ref[k] = dot_t(unit, full_ref[pl.ds(at, C), :])


def border(count):
    up = [(i, i + 1) for i in range(count - 1)]
    return up, [(b, a) for a, b in up]


def local(volume, first_filters, second_filters, out_grad):
    chan, slab, core = (lax.axis_index(a) for a in ("chan", "slab", "core"))
    place = jnp.stack([chan, slab * 2 + core, core]).astype(jnp.int32)
    swap = [(0, 1), (1, 0)]
    up, down = border(16)
    xup, xdown = border(8)
    space = ("slab", "core")

    pick = np.zeros((176, 128), np.float32)
    for c in range(8):
        for j in range(22):
            if 0 <= 16 * c - 3 + j < 128:
                pick[c * 22 + j, 16 * c - 3 + j] = 1.0
    og = out_grad.reshape(BX, BY * NZ, C)
    gxl = lax.ppermute(og[BX - 1 :], "chan", xup)
    gxh = lax.ppermute(og[:1], "chan", xdown)
    packed = pl.pallas_call(
        pack_kernel,
        out_shape=jax.ShapeDtypeStruct((176 * 16, 128), BF),
        in_specs=[VMEM, VMEM],
        out_specs=VMEM,
        scratch_shapes=[pltpu.VMEM((176 * 16, 128), F32)],
        compiler_params=params(12),
        cost_estimate=cost(16 * 176 * 128 * 256, 3 << 20),
        name="pack",
    )(jnp.asarray(pick, BF), jnp.transpose(volume, (1, 2, 3, 0)))
    near = lax.all_to_all(packed.reshape(8, 352, 128), "chan", 0, 0, tiled=True)

    w1 = jnp.transpose(first_filters, (0, 1, 2, 4, 3)).reshape(27, 32, C)
    half = lax.dynamic_slice_in_dim(w1, core * 128, 128, axis=2)
    spread = jnp.broadcast_to(half.reshape(1, 864, 128), (8, 864, 128))
    spread, near = lax.optimization_barrier((spread, near))
    pieces = lax.all_to_all(spread, "chan", 0, 0, tiled=True)

    top = jnp.concatenate([gxl[:, 56:], og[:, 56:], gxh[:, 56:]], axis=0)
    bottom = jnp.concatenate([gxl[:, :8], og[:, :8], gxh[:, :8]], axis=0)
    gyl = lax.ppermute(top, space, up)
    gyh = lax.ppermute(bottom, space, down)
    near, gyl, gyh = lax.optimization_barrier((near, gyl, gyh))
    near = near.reshape(8, 22, 16, 128)
    low = lax.ppermute(near[:, :, 8:], space, up)
    high = lax.ppermute(near[:, :, :8], space, down)
    v3 = pl.pallas_call(
        unpack_kernel,
        out_shape=jax.ShapeDtypeStruct((22, 112, 3 * C), BF),
        in_specs=[SMEM, VMEM, VMEM, VMEM],
        out_specs=VMEM,
        compiler_params=params(24),
        cost_estimate=cost(1.5e9, 6 << 20),
        name="unpack",
    )(place, near, low, high)
    v3, pieces = lax.optimization_barrier((v3, pieces))

    mine = pl.pallas_call(
        turn_kernel,
        out_shape=jax.ShapeDtypeStruct((27, 128, C), BF),
        in_specs=[VMEM],
        out_specs=VMEM,
        compiler_params=params(12),
        cost_estimate=cost(1e9, 4 << 20),
        name="turn",
    )(pieces.reshape(8, 27, 32, 128))
    other = lax.ppermute(mine, "core", swap)

    w2 = second_filters.reshape(9, 3 * C, C)
    keep, send, d3 = pl.pallas_call(
        layers_kernel,
        out_shape=(
            jax.ShapeDtypeStruct((SLOT, C), BF),
            jax.ShapeDtypeStruct((SLOT, C), BF),
            jax.ShapeDtypeStruct((18, 80, 3 * C), BF),
        ),
        in_specs=[SMEM] + [VMEM] * 9,
        out_specs=(VMEM, VMEM, VMEM),
        scratch_shapes=[
            pltpu.VMEM((20, 96, 3 * C), BF),
            pltpu.VMEM((480, C), F32),
            pltpu.VMEM((18, 80, C), BF),
            pltpu.VMEM((C, 1024), BF),
            pltpu.VMEM((2 * SLOT, C), BF),
        ],
        compiler_params=params(44),
        cost_estimate=cost(16e9, 20 << 20),
        name="layers",
    )(place, v3, mine, other, w2, og, gxl, gxh, gyl, gyh)

    w2_back = pl.pallas_call(
        flip_kernel,
        out_shape=jax.ShapeDtypeStruct((9, 3 * C, C), BF),
        in_specs=[VMEM],
        out_specs=VMEM,
        compiler_params=params(12),
        cost_estimate=cost(1e9, 7 << 20),
        name="flip",
    )(w2)
    received = lax.ppermute(send, "core", swap)
    act_grad = pl.pallas_call(
        back_kernel,
        out_shape=jax.ShapeDtypeStruct((BX, BY * NZ, C), BF),
        in_specs=[VMEM, VMEM],
        out_specs=VMEM,
        scratch_shapes=[pltpu.VMEM((1024, C), F32)],
        compiler_params=params(16),
        cost_estimate=cost(3.6e9, 7 << 20),
        name="back",
    )(d3, w2_back)

    both = (keep.astype(F32) + received.astype(F32)).astype(BF).reshape(64, 56, C)
    shares = lax.all_to_all(both, CHIPS, 0, 0, tiled=True)
    shares, act_grad = lax.optimization_barrier((shares, act_grad))
    scale = 1.0 / math.sqrt(128 * 128 * NZ)
    share = (jnp.sum(shares.astype(F32), axis=0) * scale).astype(BF)
    spread = lax.optimization_barrier(jnp.broadcast_to(share[None], (64, 56, C)))
    ours = lax.all_to_all(spread, CHIPS, 0, 0, tiled=True).reshape(SLOT, C)
    theirs = lax.ppermute(ours, "core", swap)
    whole = pl.BlockSpec((SLOT, C), lambda t: (0, 0))
    filter_grad = pl.pallas_call(
        finish_kernel,
        grid=(9,),
        out_shape=jax.ShapeDtypeStruct((27, C, C), F32),
        in_specs=[SMEM, whole, whole],
        out_specs=pl.BlockSpec((3, C, C), lambda t: (t, 0, 0)),
        scratch_shapes=[pltpu.VMEM((2 * HALF, C), BF)],
        compiler_params=params(20),
        cost_estimate=cost(1e9, 11 << 20),
        name="finish",
    )(place, ours, theirs)
    return (
        act_grad.reshape(BX, BY, NZ, C),
        filter_grad.reshape(3, 3, 3, C, C),
    )


def solution(mesh):
    cells = Mesh(mesh.devices.reshape(8, 8, 2), ("chan", "slab", "core"))
    space = ("slab", "core")
    placed = (
        P(None, space, None, "chan"),
        P(None, None, None, None, "chan"),
        P(),
        P("chan", space, None, None),
    )
    return jax.shard_map(
        local,
        mesh=cells,
        in_specs=placed,
        out_specs=(P("chan", space, None, None), P()),
        check_vma=False,
    )
```

```python
import functools
import math

import jax
import jax.numpy as jnp
from jax import lax
from jax.experimental import pallas as pl
from jax.experimental.pallas import tpu as pltpu
from jax.sharding import Mesh
from jax.sharding import PartitionSpec as P

BF = jnp.bfloat16
F32 = jnp.float32
C = 256
NZ = 8
BX, BY = 16, 8
TAPS = 14
SLOT = TAPS * C
VOL = 352
STRAIGHT = 15
QUARTER = (27 - STRAIGHT) // 4
CHIPS = ("chan", "slab")
VMEM = pl.BlockSpec(memory_space=pltpu.VMEM)
SMEM = pl.BlockSpec(memory_space=pltpu.SMEM)


def params(mib):
    return pltpu.CompilerParams(vmem_limit_bytes=mib << 20)


def cost(flops, moved):
    return pl.CostEstimate(flops=int(flops), bytes_accessed=int(moved), transcendentals=0)


def dot_t(a, b):
    return lax.dot_general(a, b, (((1,), (1,)), ((), ())), preferred_element_type=F32)


def dot_n(a, b):
    return lax.dot_general(a, b, (((1,), (0,)), ((), ())), preferred_element_type=F32)


def pack_kernel(place_ref, vol_ref, filters_ref, out_ref, straight_ref, wide_ref):
    row = lax.broadcasted_iota(jnp.int32, (176, 128), 0)
    col = lax.broadcasted_iota(jnp.int32, (176, 128), 1)
    c = sum((row >= 22 * n).astype(jnp.int32) for n in range(1, 8))
    pick = (col == row - 6 * c - 3).astype(F32).astype(BF)
    for quad in range(2):
        for z in range(NZ):
            rows = jnp.concatenate([vol_ref[quad * 4 + j, z] for j in range(4)], axis=0)
            wide_ref[quad, pl.ds(z, 176, stride=8), :] = dot_t(pick, rows)
    lanes = pl.ds(pl.multiple_of(place_ref[2] * 128, 128), 128)
    mine = pl.ds(STRAIGHT + QUARTER * place_ref[3], QUARTER)
    quarter = filters_ref[mine, :, lanes].reshape(QUARTER * 32, 128)
    straight = filters_ref[0:STRAIGHT, :, lanes].reshape(STRAIGHT * 32, 128)
    for c in range(8):
        for quad in range(2):
            part = wide_ref[quad, c * 176 : c * 176 + 176, :]
            out_ref[c, quad * 176 : quad * 176 + 176, :] = part.astype(BF)
        out_ref[c, VOL : VOL + QUARTER * 32, :] = quarter
        straight_ref[c] = straight


def neighbours(value):
    z = lax.broadcasted_iota(jnp.int32, value.shape, 1)
    before = jnp.where(z == 0, 0.0, pltpu.roll(value, 1, 1))
    after = jnp.where(z == NZ - 1, 0.0, pltpu.roll(value, NZ - 1, 1))
    return before.astype(BF), after.astype(BF)


def unpack_kernel(place_ref, near_ref, low_ref, high_ref, v3_ref):
    core = place_ref[2]
    row = lax.broadcasted_iota(jnp.int32, (1024, C), 0)
    col = lax.broadcasted_iota(jnp.int32, (1024, C), 1) ^ (core * 128)
    same = ((row >> 7) == (col >> 5)) & ((row & 31) == (col & 31))
    for j in range(4):
        sel = (same & (((row >> 5) & 3) == j)).astype(F32).astype(BF)
        for b in range(4):
            y = b * 4 + j - 1
            if y < 0 or y >= 14:
                continue
            src = (low_ref, near_ref, near_ref, high_ref)[b]
            at = 176 if b == 2 else 0
            rows = jnp.concatenate([src[c, at : at + 176, :] for c in range(8)], axis=1)
            value = dot_n(rows, sel).reshape(22, NZ, C)
            before, after = neighbours(value)
            v3_ref[:, y * 8 : y * 8 + 8, 0:C] = before
            v3_ref[:, y * 8 : y * 8 + 8, C : 2 * C] = value.astype(BF)
            v3_ref[:, y * 8 : y * 8 + 8, 2 * C : 3 * C] = after


def turn_kernel(place_ref, near_ref, q1_ref, q2_ref, q3_ref, straight_ref, out_ref):
    def turn(t, carry):
        at = pl.ds(pl.multiple_of(t * 32, 32), 32)
        rows = jnp.concatenate([straight_ref[c, at, :] for c in range(8)], axis=0)
        out_ref[t] = rows.T
        return carry

    lax.fori_loop(0, STRAIGHT, turn, 0)
    for d, ref in enumerate((near_ref, q1_ref, q2_ref, q3_ref)):
        first = STRAIGHT + QUARTER * lax.rem(place_ref[3] - d + 4, 4)
        for k in range(QUARTER):
            at = k * 32 + (VOL if d == 0 else 0)
            rows = jnp.concatenate([ref[c, at : at + 32, :] for c in range(8)], axis=0)
            out_ref[first + k] = rows.T


def layers_kernel(
    place_ref, v3_ref, mine_ref, other_ref, w2_ref,
    grad_ref, gxl_ref, gxh_ref, gyl_ref, gyh_ref,
    keep_ref, send_ref, d3_ref,
    a3_ref, acc_ref, og_ref, dt_ref, g_ref,
):
    chan, space, core = place_ref[0], place_ref[1], place_ref[2]

    def first(i, carry):
        x0 = i * 5
        for s in range(9):
            part = v3_ref[pl.ds(x0 + s // 3, 5), (s % 3) * 8 : (s % 3) * 8 + 96, :]
            w = [h[3 * s + k] for k in range(3) for h in (mine_ref, other_ref)]
            part = dot_n(part.reshape(480, 3 * C), jnp.concatenate(w, axis=0))
            if s == 0:
                acc_ref[...] = part
            else:
                acc_ref[...] += part
        v = acc_ref[...]
        act = (v / (1.0 + jnp.exp(-v))).astype(BF)
        wide = act.astype(F32).reshape(60, NZ, C)
        before, after = neighbours(wide)
        a3_ref[pl.ds(x0, 5), :, 0:C] = before.reshape(5, 96, C)
        a3_ref[pl.ds(x0, 5), :, C : 2 * C] = act.reshape(5, 96, C)
        a3_ref[pl.ds(x0, 5), :, 2 * C : 3 * C] = after.reshape(5, 96, C)
        return carry

    lax.fori_loop(0, 4, first, 0)

    @pl.when(chan == 0)
    def _():
        a3_ref[0:2] = jnp.zeros((2, 96, 3 * C), BF)

    @pl.when(chan == 7)
    def _():
        a3_ref[18:20] = jnp.zeros((2, 96, 3 * C), BF)

    @pl.when(space == 0)
    def _():
        a3_ref[:, 0:16, :] = jnp.zeros((20, 16, 3 * C), BF)

    @pl.when(space == 15)
    def _():
        a3_ref[:, 80:96, :] = jnp.zeros((20, 16, 3 * C), BF)

    og_ref[1:17, 8:72, :] = grad_ref[...]
    og_ref[0:1, 8:72, :] = gxl_ref[...]
    og_ref[17:18, 8:72, :] = gxh_ref[...]
    og_ref[:, 0:8, :] = gyl_ref[...]
    og_ref[:, 72:80, :] = gyh_ref[...]

    def second(i, carry):
        x0 = i * 6
        for s in range(9):
            part = a3_ref[pl.ds(x0 + s // 3, 6), (s % 3) * 8 : (s % 3) * 8 + 80, :]
            part = dot_n(part.reshape(480, 3 * C), w2_ref[s])
            if s == 0:
                acc_ref[...] = part
            else:
                acc_ref[...] += part
        v = acc_ref[...]
        sig = 1.0 / (1.0 + jnp.exp(-v))
        og = og_ref[pl.ds(x0, 6)].reshape(480, C).astype(F32)
        delta = (og * sig * (1.0 + v * (1.0 - sig))).astype(BF)
        before, after = neighbours(delta.astype(F32).reshape(60, NZ, C))
        d3_ref[pl.ds(x0, 6), :, 0:C] = after.reshape(6, 80, C)
        d3_ref[pl.ds(x0, 6), :, C : 2 * C] = delta.reshape(6, 80, C)
        d3_ref[pl.ds(x0, 6), :, 2 * C : 3 * C] = before.reshape(6, 80, C)
        return carry

    lax.fori_loop(0, 3, second, 0)

    dt_ref[...] = d3_ref[1:17, 8:72, C : 2 * C].reshape(1024, C).T
    for s in range(9):
        part = a3_ref[1 + s // 3 : 17 + s // 3, (1 + s % 3) * 8 : (1 + s % 3) * 8 + 64, :]
        g = dot_n(dt_ref[...], part.reshape(1024, 3 * C)).astype(BF)
        for tz in range(3):
            t = 3 * s + tz
            g_ref[t * C : (t + 1) * C, :] = g[:, tz * C : (tz + 1) * C]
    g_ref[27 * C : 28 * C, :] = jnp.zeros((C, C), BF)
    keep_ref[...] = g_ref[pl.ds(pl.multiple_of(core * SLOT, 16), SLOT), :]
    send_ref[...] = g_ref[pl.ds(pl.multiple_of((1 - core) * SLOT, 16), SLOT), :]


def flip_kernel(w_ref, out_ref):
    def turn(s, carry):
        for k in range(3):
            out_ref[s, k * C : (k + 1) * C, :] = w_ref[s, k * C : (k + 1) * C, :].T
        return carry

    lax.fori_loop(0, 9, turn, 0)


def back_kernel(d3_ref, w2_ref, out_ref, acc_ref):
    for s in range(9):
        tx, ty = s // 3, s % 3
        part = d3_ref[2 - tx : 18 - tx, (2 - ty) * 8 : (2 - ty) * 8 + 64, :]
        part = dot_n(part.reshape(1024, 3 * C), w2_ref[s])
        if s == 0:
            acc_ref[...] = part
        elif s < 8:
            acc_ref[...] += part
        else:
            out_ref[...] = (acc_ref[...] + part).astype(BF).reshape(BX, 64, C)


def finish_kernel(own, place_ref, sums_ref, *refs):
    out_ref, tile_ref, sems = refs[-3:]
    half = place_ref[2] if own else 1 - place_ref[2]
    count = TAPS - half

    def copy(t):
        return pltpu.make_async_copy(
            tile_ref.at[t], out_ref.at[half * TAPS + t], sems.at[t]
        )

    def turn(t, carry):
        at = pl.multiple_of(t * C, C)
        tile_ref[t] = sums_ref[pl.ds(at, C), :].T.astype(F32)
        copy(t).start()
        return carry

    def wait(t, carry):
        copy(t).wait()
        return carry

    lax.fori_loop(0, count, turn, 0)
    lax.fori_loop(0, count, wait, 0)


def border(count):
    up = [(i, i + 1) for i in range(count - 1)]
    return up, [(b, a) for a, b in up]


def local(volume, first_filters, second_filters, out_grad):
    chan, slab, core = (lax.axis_index(a) for a in ("chan", "slab", "core"))
    along_y = lax.rem(slab, 4)
    place = jnp.stack([chan, slab * 2 + core, core, along_y]).astype(jnp.int32)
    swap = [(0, 1), (1, 0)]
    up, down = border(16)
    xup, xdown = border(8)
    space = ("slab", "core")

    og = out_grad.reshape(BX, BY * NZ, C)
    gxl = lax.ppermute(og[BX - 1 :], "chan", xup)
    gxh = lax.ppermute(og[:1], "chan", xdown)

    packed, straight = pl.pallas_call(
        pack_kernel,
        out_shape=(
            jax.ShapeDtypeStruct((8, VOL + QUARTER * 32, 128), BF),
            jax.ShapeDtypeStruct((8, STRAIGHT * 32, 128), BF),
        ),
        in_specs=[SMEM, VMEM, VMEM],
        out_specs=(VMEM, VMEM),
        scratch_shapes=[pltpu.VMEM((2, 8 * 176, 128), F32)],
        compiler_params=params(16),
        cost_estimate=cost(16 * 176 * 128 * 256, 3 << 20),
        name="pack",
    )(
        place,
        jnp.transpose(volume, (1, 2, 3, 0)),
        jnp.transpose(first_filters, (0, 1, 2, 4, 3)).reshape(27, 32, C),
    )
    near = lax.all_to_all(packed, "chan", 0, 0, tiled=True)

    w2 = second_filters.reshape(9, 3 * C, C)
    near, gxl, gxh, straight = lax.optimization_barrier((near, gxl, gxh, straight))
    straight = lax.all_to_all(straight, "chan", 0, 0, tiled=True)
    quarters = [
        lax.ppermute(
            near[:, VOL:],
            "slab",
            [(z + y, z + (y + d) % 4) for z in (0, 4) for y in range(4)],
        )
        for d in range(1, 4)
    ]

    top = jnp.concatenate([gxl[:, 56:], og[:, 56:], gxh[:, 56:]], axis=0)
    bottom = jnp.concatenate([gxl[:, :8], og[:, :8], gxh[:, :8]], axis=0)
    gyl = lax.ppermute(top, space, up)
    gyh = lax.ppermute(bottom, space, down)
    low = lax.ppermute(near[:, 176:VOL], space, up)
    high = lax.ppermute(near[:, :176], space, down)
    w2_back = pl.pallas_call(
        flip_kernel,
        out_shape=jax.ShapeDtypeStruct((9, 3 * C, C), BF),
        in_specs=[VMEM],
        out_specs=VMEM,
        compiler_params=params(12),
        cost_estimate=cost(1e9, 7 << 20),
        name="flip",
    )(w2)
    w2_back, gyl, gyh, low, high, straight = lax.optimization_barrier(
        (w2_back, gyl, gyh, low, high, straight)
    )
    v3 = pl.pallas_call(
        unpack_kernel,
        out_shape=jax.ShapeDtypeStruct((22, 112, 3 * C), BF),
        in_specs=[SMEM, VMEM, VMEM, VMEM],
        out_specs=VMEM,
        compiler_params=params(16),
        cost_estimate=cost(1.5e9, 6 << 20),
        name="unpack",
    )(place, near, low, high)

    mine = pl.pallas_call(
        turn_kernel,
        out_shape=jax.ShapeDtypeStruct((27, 128, C), BF),
        in_specs=[SMEM] + [VMEM] * 5,
        out_specs=VMEM,
        compiler_params=params(12),
        cost_estimate=cost(1e9, 4 << 20),
        name="turn",
    )(place, near, *quarters, straight)
    other = lax.ppermute(mine, "core", swap)

    keep, send, d3 = pl.pallas_call(
        layers_kernel,
        out_shape=(
            jax.ShapeDtypeStruct((SLOT, C), BF),
            jax.ShapeDtypeStruct((SLOT, C), BF),
            jax.ShapeDtypeStruct((18, 80, 3 * C), BF),
        ),
        in_specs=[SMEM] + [VMEM] * 9,
        out_specs=(VMEM, VMEM, VMEM),
        scratch_shapes=[
            pltpu.VMEM((20, 96, 3 * C), BF),
            pltpu.VMEM((480, C), F32),
            pltpu.VMEM((18, 80, C), BF),
            pltpu.VMEM((C, 1024), BF),
            pltpu.VMEM((2 * SLOT, C), BF),
        ],
        compiler_params=params(30),
        cost_estimate=cost(16e9, 20 << 20),
        name="layers",
    )(place, v3, mine, other, w2, og, gxl, gxh, gyl, gyh)

    received = lax.ppermute(send, "core", swap)
    act_grad = pl.pallas_call(
        back_kernel,
        out_shape=jax.ShapeDtypeStruct((BX, BY * NZ, C), BF),
        in_specs=[VMEM, VMEM],
        out_specs=VMEM,
        scratch_shapes=[pltpu.VMEM((1024, C), F32)],
        compiler_params=params(16),
        cost_estimate=cost(3.6e9, 7 << 20),
        name="back",
    )(d3, w2_back)

    received, act_grad = lax.optimization_barrier((received, act_grad))
    both = (keep.astype(F32) + received.astype(F32)).astype(BF).reshape(64, 56, C)
    shares = lax.all_to_all(both, CHIPS, 0, 0, tiled=True)
    scale = 1.0 / math.sqrt(128 * 128 * NZ)
    share = (jnp.sum(shares.astype(F32), axis=0) * scale).astype(BF)
    spread = lax.optimization_barrier(jnp.broadcast_to(share[None], (64, 56, C)))
    ours = lax.all_to_all(spread, CHIPS, 0, 0, tiled=True).reshape(SLOT, C)
    theirs = lax.ppermute(ours, "core", swap)
    anywhere = pl.BlockSpec(memory_space=pl.ANY)

    def finish(own, *operands):
        return pl.pallas_call(
            functools.partial(finish_kernel, own),
            out_shape=jax.ShapeDtypeStruct((27, C, C), F32),
            in_specs=[SMEM, VMEM] + [anywhere] * (len(operands) - 2),
            out_specs=anywhere,
            scratch_shapes=[pltpu.VMEM((TAPS, C, C), F32), pltpu.SemaphoreType.DMA((TAPS,))],
            input_output_aliases={2: 0} if len(operands) > 2 else {},
            compiler_params=params(12),
            cost_estimate=cost(1e9, 5 << 20),
            name="finish",
        )(*operands)

    filter_grad = finish(True, place, ours)
    filter_grad = finish(False, place, theirs, filter_grad)
    return (
        act_grad.reshape(BX, BY, NZ, C),
        filter_grad.reshape(3, 3, 3, C, C),
    )


def solution(mesh):
    cells = Mesh(mesh.devices.reshape(8, 8, 2), ("chan", "slab", "core"))
    space = ("slab", "core")
    placed = (
        P(None, space, None, "chan"),
        P(None, None, None, None, "chan"),
        P(),
        P("chan", space, None, None),
    )
    return jax.shard_map(
        local,
        mesh=cells,
        in_specs=placed,
        out_specs=(P("chan", space, None, None), P()),
        check_vma=False,
    )
```

```python
import functools
import math

import jax
import jax.numpy as jnp
from jax import lax
from jax.experimental import pallas as pl
from jax.experimental.pallas import tpu as pltpu
from jax.sharding import Mesh
from jax.sharding import PartitionSpec as P

BF = jnp.bfloat16
F32 = jnp.float32
C = 256
NZ = 8
BX, BY = 16, 8
TAPS = 14
SLOT = TAPS * C
VOL = 352
STRAIGHT = 15
QUARTER = (27 - STRAIGHT) // 4
CHIPS = ("chan", "slab")
VMEM = pl.BlockSpec(memory_space=pltpu.VMEM)
SMEM = pl.BlockSpec(memory_space=pltpu.SMEM)


def params(mib):
    return pltpu.CompilerParams(vmem_limit_bytes=mib << 20)


def cost(flops, moved):
    return pl.CostEstimate(flops=int(flops), bytes_accessed=int(moved), transcendentals=0)


def dot_t(a, b):
    return lax.dot_general(a, b, (((1,), (1,)), ((), ())), preferred_element_type=F32)


def dot_n(a, b):
    return lax.dot_general(a, b, (((1,), (0,)), ((), ())), preferred_element_type=F32)


def pack_kernel(place_ref, vol_ref, filters_ref, out_ref, straight_ref, wide_ref):
    row = lax.broadcasted_iota(jnp.int32, (176, 128), 0)
    col = lax.broadcasted_iota(jnp.int32, (176, 128), 1)
    c = sum((row >= 22 * n).astype(jnp.int32) for n in range(1, 8))
    pick = (col == row - 6 * c - 3).astype(F32).astype(BF)
    for quad in range(2):
        for z in range(NZ):
            rows = jnp.concatenate([vol_ref[quad * 4 + j, z] for j in range(4)], axis=0)
            wide_ref[quad, pl.ds(z, 176, stride=8), :] = dot_t(pick, rows)
    lanes = pl.ds(pl.multiple_of(place_ref[2] * 128, 128), 128)
    mine = pl.ds(STRAIGHT + QUARTER * place_ref[3], QUARTER)
    quarter = filters_ref[mine, :, lanes].reshape(QUARTER * 32, 128)
    straight = filters_ref[0:STRAIGHT, :, lanes].reshape(STRAIGHT * 32, 128)
    for c in range(8):
        for quad in range(2):
            part = wide_ref[quad, c * 176 : c * 176 + 176, :]
            out_ref[c, quad * 176 : quad * 176 + 176, :] = part.astype(BF)
        out_ref[c, VOL : VOL + QUARTER * 32, :] = quarter
        straight_ref[c] = straight


def neighbours(value):
    z = lax.broadcasted_iota(jnp.int32, value.shape, 1)
    before = jnp.where(z == 0, 0.0, pltpu.roll(value, 1, 1))
    after = jnp.where(z == NZ - 1, 0.0, pltpu.roll(value, NZ - 1, 1))
    return before.astype(BF), after.astype(BF)


def unpack_kernel(place_ref, near_ref, low_ref, high_ref, v3_ref):
    core = place_ref[2]
    row = lax.broadcasted_iota(jnp.int32, (1024, C), 0)
    col = lax.broadcasted_iota(jnp.int32, (1024, C), 1) ^ (core * 128)
    same = ((row >> 7) == (col >> 5)) & ((row & 31) == (col & 31))
    for j in range(4):
        sel = (same & (((row >> 5) & 3) == j)).astype(F32).astype(BF)
        for b in range(4):
            y = b * 4 + j - 1
            if y < 0 or y >= 14:
                continue
            src = (low_ref, near_ref, near_ref, high_ref)[b]
            at = 176 if b == 2 else 0
            rows = jnp.concatenate([src[c, at : at + 176, :] for c in range(8)], axis=1)
            value = dot_n(rows, sel).reshape(22, NZ, C)
            before, after = neighbours(value)
            v3_ref[:, y * 8 : y * 8 + 8, 0:C] = before
            v3_ref[:, y * 8 : y * 8 + 8, C : 2 * C] = value.astype(BF)
            v3_ref[:, y * 8 : y * 8 + 8, 2 * C : 3 * C] = after


def turn_kernel(place_ref, near_ref, q1_ref, q2_ref, q3_ref, straight_ref, out_ref):
    def turn(t, carry):
        at = pl.ds(pl.multiple_of(t * 32, 32), 32)
        rows = jnp.concatenate([straight_ref[c, at, :] for c in range(8)], axis=0)
        out_ref[t] = rows.T
        return carry

    lax.fori_loop(0, STRAIGHT, turn, 0)
    for d, ref in enumerate((near_ref, q1_ref, q2_ref, q3_ref)):
        first = STRAIGHT + QUARTER * lax.rem(place_ref[3] - d + 4, 4)
        for k in range(QUARTER):
            at = k * 32 + (VOL if d == 0 else 0)
            rows = jnp.concatenate([ref[c, at : at + 32, :] for c in range(8)], axis=0)
            out_ref[first + k] = rows.T


def layers_kernel(
    place_ref, v3_ref, mine_ref, other_ref, w2_ref,
    grad_ref, gxl_ref, gxh_ref, gyl_ref, gyh_ref,
    keep_ref, send_ref, d3_ref,
    a3_ref, acc_ref, og_ref, dt_ref, g_ref,
):
    chan, space, core = place_ref[0], place_ref[1], place_ref[2]

    def first(i, carry):
        x0 = i * 5
        for s in range(9):
            part = v3_ref[pl.ds(x0 + s // 3, 5), (s % 3) * 8 : (s % 3) * 8 + 96, :]
            w = [h[3 * s + k] for k in range(3) for h in (mine_ref, other_ref)]
            part = dot_n(part.reshape(480, 3 * C), jnp.concatenate(w, axis=0))
            if s == 0:
                acc_ref[...] = part
            else:
                acc_ref[...] += part
        v = acc_ref[...]
        act = (v / (1.0 + jnp.exp(-v))).astype(BF)
        wide = act.astype(F32).reshape(60, NZ, C)
        before, after = neighbours(wide)
        a3_ref[pl.ds(x0, 5), :, 0:C] = before.reshape(5, 96, C)
        a3_ref[pl.ds(x0, 5), :, C : 2 * C] = act.reshape(5, 96, C)
        a3_ref[pl.ds(x0, 5), :, 2 * C : 3 * C] = after.reshape(5, 96, C)
        return carry

    lax.fori_loop(0, 4, first, 0)

    @pl.when(chan == 0)
    def _():
        a3_ref[0:2] = jnp.zeros((2, 96, 3 * C), BF)

    @pl.when(chan == 7)
    def _():
        a3_ref[18:20] = jnp.zeros((2, 96, 3 * C), BF)

    @pl.when(space == 0)
    def _():
        a3_ref[:, 0:16, :] = jnp.zeros((20, 16, 3 * C), BF)

    @pl.when(space == 15)
    def _():
        a3_ref[:, 80:96, :] = jnp.zeros((20, 16, 3 * C), BF)

    og_ref[1:17, 8:72, :] = grad_ref[...]
    og_ref[0:1, 8:72, :] = gxl_ref[...]
    og_ref[17:18, 8:72, :] = gxh_ref[...]
    og_ref[:, 0:8, :] = gyl_ref[...]
    og_ref[:, 72:80, :] = gyh_ref[...]

    def second(i, carry):
        x0 = i * 6
        for s in range(9):
            part = a3_ref[pl.ds(x0 + s // 3, 6), (s % 3) * 8 : (s % 3) * 8 + 80, :]
            part = dot_n(part.reshape(480, 3 * C), w2_ref[s])
            if s == 0:
                acc_ref[...] = part
            else:
                acc_ref[...] += part
        v = acc_ref[...]
        sig = 1.0 / (1.0 + jnp.exp(-v))
        og = og_ref[pl.ds(x0, 6)].reshape(480, C).astype(F32)
        delta = (og * sig * (1.0 + v * (1.0 - sig))).astype(BF)
        before, after = neighbours(delta.astype(F32).reshape(60, NZ, C))
        d3_ref[pl.ds(x0, 6), :, 0:C] = after.reshape(6, 80, C)
        d3_ref[pl.ds(x0, 6), :, C : 2 * C] = delta.reshape(6, 80, C)
        d3_ref[pl.ds(x0, 6), :, 2 * C : 3 * C] = before.reshape(6, 80, C)
        return carry

    lax.fori_loop(0, 3, second, 0)

    dt_ref[...] = d3_ref[1:17, 8:72, C : 2 * C].reshape(1024, C).T
    for s in range(9):
        part = a3_ref[1 + s // 3 : 17 + s // 3, (1 + s % 3) * 8 : (1 + s % 3) * 8 + 64, :]
        g = dot_n(dt_ref[...], part.reshape(1024, 3 * C)).astype(BF)
        for tz in range(3):
            t = 3 * s + tz
            g_ref[t * C : (t + 1) * C, :] = g[:, tz * C : (tz + 1) * C]
    g_ref[27 * C : 28 * C, :] = jnp.zeros((C, C), BF)
    keep_ref[...] = g_ref[pl.ds(pl.multiple_of(core * SLOT, 16), SLOT), :]
    send_ref[...] = g_ref[pl.ds(pl.multiple_of((1 - core) * SLOT, 16), SLOT), :]


def flip_kernel(w_ref, out_ref):
    def turn(s, carry):
        for k in range(3):
            out_ref[s, k * C : (k + 1) * C, :] = w_ref[s, k * C : (k + 1) * C, :].T
        return carry

    lax.fori_loop(0, 9, turn, 0)


def back_kernel(d3_ref, w2_ref, out_ref, acc_ref):
    for s in range(9):
        tx, ty = s // 3, s % 3
        part = d3_ref[2 - tx : 18 - tx, (2 - ty) * 8 : (2 - ty) * 8 + 64, :]
        part = dot_n(part.reshape(1024, 3 * C), w2_ref[s])
        if s == 0:
            acc_ref[...] = part
        elif s < 8:
            acc_ref[...] += part
        else:
            out_ref[...] = (acc_ref[...] + part).astype(BF).reshape(BX, 64, C)


def finish_kernel(own, place_ref, sums_ref, *refs):
    out_ref, tile_ref, sems = refs[-3:]
    half = place_ref[2] if own else 1 - place_ref[2]
    count = TAPS - half

    def copy(t):
        return pltpu.make_async_copy(
            tile_ref.at[t], out_ref.at[half * TAPS + t], sems.at[t]
        )

    def turn(t, carry):
        at = pl.multiple_of(t * C, C)
        tile_ref[t] = sums_ref[pl.ds(at, C), :].T.astype(F32)
        copy(t).start()
        return carry

    def wait(t, carry):
        copy(t).wait()
        return carry

    lax.fori_loop(0, count, turn, 0)
    lax.fori_loop(0, count, wait, 0)


def border(count):
    up = [(i, i + 1) for i in range(count - 1)]
    return up, [(b, a) for a, b in up]


def local(volume, first_filters, second_filters, out_grad):
    chan, slab, core = (lax.axis_index(a) for a in ("chan", "slab", "core"))
    along_y = lax.rem(slab, 4)
    place = jnp.stack([chan, slab * 2 + core, core, along_y]).astype(jnp.int32)
    swap = [(0, 1), (1, 0)]
    up, down = border(16)
    xup, xdown = border(8)
    space = ("slab", "core")

    og = out_grad.reshape(BX, BY * NZ, C)
    gxl = lax.ppermute(og[BX - 1 :], "chan", xup)
    gxh = lax.ppermute(og[:1], "chan", xdown)

    packed, straight = pl.pallas_call(
        pack_kernel,
        out_shape=(
            jax.ShapeDtypeStruct((8, VOL + QUARTER * 32, 128), BF),
            jax.ShapeDtypeStruct((8, STRAIGHT * 32, 128), BF),
        ),
        in_specs=[SMEM, VMEM, VMEM],
        out_specs=(VMEM, VMEM),
        scratch_shapes=[pltpu.VMEM((2, 8 * 176, 128), F32)],
        compiler_params=params(16),
        cost_estimate=cost(16 * 176 * 128 * 256, 3 << 20),
        name="pack",
    )(
        place,
        jnp.transpose(volume, (1, 2, 3, 0)),
        jnp.transpose(first_filters, (0, 1, 2, 4, 3)).reshape(27, 32, C),
    )
    near = lax.all_to_all(packed, "chan", 0, 0, tiled=True)

    w2 = second_filters.reshape(9, 3 * C, C)
    w2_back = pl.pallas_call(
        flip_kernel,
        out_shape=jax.ShapeDtypeStruct((9, 3 * C, C), BF),
        in_specs=[VMEM],
        out_specs=VMEM,
        compiler_params=params(12),
        cost_estimate=cost(1e9, 7 << 20),
        name="flip",
    )(w2)
    near, gxl, gxh, straight, w2_back = lax.optimization_barrier(
        (near, gxl, gxh, straight, w2_back)
    )
    straight = lax.all_to_all(straight, "chan", 0, 0, tiled=True)
    quarters = [
        lax.ppermute(
            near[:, VOL:],
            "slab",
            [(z + y, z + (y + d) % 4) for z in (0, 4) for y in range(4)],
        )
        for d in range(1, 4)
    ]

    low = lax.ppermute(near[:, 176:VOL], space, up)
    high = lax.ppermute(near[:, :176], space, down)
    low, high, gxl, gxh = lax.optimization_barrier((low, high, gxl, gxh))

    top = jnp.concatenate([gxl[:, 56:], og[:, 56:], gxh[:, 56:]], axis=0)
    bottom = jnp.concatenate([gxl[:, :8], og[:, :8], gxh[:, :8]], axis=0)
    gyl = lax.ppermute(top, space, up)
    gyh = lax.ppermute(bottom, space, down)
    gyl, gyh, low, high, straight = lax.optimization_barrier((gyl, gyh, low, high, straight))
    v3 = pl.pallas_call(
        unpack_kernel,
        out_shape=jax.ShapeDtypeStruct((22, 112, 3 * C), BF),
        in_specs=[SMEM, VMEM, VMEM, VMEM],
        out_specs=VMEM,
        compiler_params=params(16),
        cost_estimate=cost(1.5e9, 6 << 20),
        name="unpack",
    )(place, near, low, high)

    mine = pl.pallas_call(
        turn_kernel,
        out_shape=jax.ShapeDtypeStruct((27, 128, C), BF),
        in_specs=[SMEM] + [VMEM] * 5,
        out_specs=VMEM,
        compiler_params=params(12),
        cost_estimate=cost(1e9, 4 << 20),
        name="turn",
    )(place, near, *quarters, straight)
    other = lax.ppermute(mine, "core", swap)

    keep, send, d3 = pl.pallas_call(
        layers_kernel,
        out_shape=(
            jax.ShapeDtypeStruct((SLOT, C), BF),
            jax.ShapeDtypeStruct((SLOT, C), BF),
            jax.ShapeDtypeStruct((18, 80, 3 * C), BF),
        ),
        in_specs=[SMEM] + [VMEM] * 9,
        out_specs=(VMEM, VMEM, VMEM),
        scratch_shapes=[
            pltpu.VMEM((20, 96, 3 * C), BF),
            pltpu.VMEM((480, C), F32),
            pltpu.VMEM((18, 80, C), BF),
            pltpu.VMEM((C, 1024), BF),
            pltpu.VMEM((2 * SLOT, C), BF),
        ],
        compiler_params=params(30),
        cost_estimate=cost(16e9, 20 << 20),
        name="layers",
    )(place, v3, mine, other, w2, og, gxl, gxh, gyl, gyh)

    received = lax.ppermute(send, "core", swap)
    act_grad = pl.pallas_call(
        back_kernel,
        out_shape=jax.ShapeDtypeStruct((BX, BY * NZ, C), BF),
        in_specs=[VMEM, VMEM],
        out_specs=VMEM,
        scratch_shapes=[pltpu.VMEM((1024, C), F32)],
        compiler_params=params(16),
        cost_estimate=cost(3.6e9, 7 << 20),
        name="back",
    )(d3, w2_back)

    received, act_grad = lax.optimization_barrier((received, act_grad))
    both = (keep.astype(F32) + received.astype(F32)).astype(BF).reshape(64, 56, C)
    shares = lax.all_to_all(both, CHIPS, 0, 0, tiled=True)
    scale = 1.0 / math.sqrt(128 * 128 * NZ)
    share = (jnp.sum(shares.astype(F32), axis=0) * scale).astype(BF)
    spread = lax.optimization_barrier(jnp.broadcast_to(share[None], (64, 56, C)))
    ours = lax.all_to_all(spread, CHIPS, 0, 0, tiled=True).reshape(SLOT, C)
    theirs = lax.ppermute(ours, "core", swap)
    anywhere = pl.BlockSpec(memory_space=pl.ANY)

    def finish(own, *operands):
        return pl.pallas_call(
            functools.partial(finish_kernel, own),
            out_shape=jax.ShapeDtypeStruct((27, C, C), F32),
            in_specs=[SMEM, VMEM] + [anywhere] * (len(operands) - 2),
            out_specs=anywhere,
            scratch_shapes=[pltpu.VMEM((TAPS, C, C), F32), pltpu.SemaphoreType.DMA((TAPS,))],
            input_output_aliases={2: 0} if len(operands) > 2 else {},
            compiler_params=params(12),
            cost_estimate=cost(1e9, 5 << 20),
            name="finish",
        )(*operands)

    filter_grad = finish(True, place, ours)
    filter_grad = finish(False, place, theirs, filter_grad)
    return (
        act_grad.reshape(BX, BY, NZ, C),
        filter_grad.reshape(3, 3, 3, C, C),
    )


def solution(mesh):
    cells = Mesh(mesh.devices.reshape(8, 8, 2), ("chan", "slab", "core"))
    space = ("slab", "core")
    placed = (
        P(None, space, None, "chan"),
        P(None, None, None, None, "chan"),
        P(),
        P("chan", space, None, None),
    )
    return jax.shard_map(
        local,
        mesh=cells,
        in_specs=placed,
        out_specs=(P("chan", space, None, None), P()),
        check_vma=False,
    )
```

```python
import functools
import math

import jax
import jax.numpy as jnp
from jax import lax
from jax.experimental import pallas as pl
from jax.experimental.pallas import tpu as pltpu
from jax.sharding import Mesh
from jax.sharding import PartitionSpec as P

BF = jnp.bfloat16
F32 = jnp.float32
C = 256
NZ = 8
BX, BY = 16, 8
TAPS = 14
SLOT = TAPS * C
VOL = 352
STRAIGHT = 15
QUARTER = (27 - STRAIGHT) // 4
CHIPS = ("chan", "slab")
VMEM = pl.BlockSpec(memory_space=pltpu.VMEM)
SMEM = pl.BlockSpec(memory_space=pltpu.SMEM)


def params(mib):
    return pltpu.CompilerParams(vmem_limit_bytes=mib << 20)


def cost(flops, moved):
    return pl.CostEstimate(flops=int(flops), bytes_accessed=int(moved), transcendentals=0)


def dot_t(a, b):
    return lax.dot_general(a, b, (((1,), (1,)), ((), ())), preferred_element_type=F32)


def dot_n(a, b):
    return lax.dot_general(a, b, (((1,), (0,)), ((), ())), preferred_element_type=F32)


def pack_kernel(place_ref, vol_ref, filters_ref, out_ref, wide_ref):
    row = lax.broadcasted_iota(jnp.int32, (176, 128), 0)
    col = lax.broadcasted_iota(jnp.int32, (176, 128), 1)
    c = sum((row >= 22 * n).astype(jnp.int32) for n in range(1, 8))
    pick = (col == row - 6 * c - 3).astype(F32).astype(BF)
    for quad in range(2):
        for z in range(NZ):
            rows = jnp.concatenate([vol_ref[quad * 4 + j, z] for j in range(4)], axis=0)
            wide_ref[quad, pl.ds(z, 176, stride=8), :] = dot_t(pick, rows)
    lanes = pl.ds(pl.multiple_of(place_ref[2] * 128, 128), 128)
    mine = pl.ds(STRAIGHT + QUARTER * place_ref[3], QUARTER)
    quarter = filters_ref[mine, :, lanes].reshape(QUARTER * 32, 128)
    for c in range(8):
        for quad in range(2):
            part = wide_ref[quad, c * 176 : c * 176 + 176, :]
            out_ref[c, quad * 176 : quad * 176 + 176, :] = part.astype(BF)
        out_ref[c, VOL : VOL + QUARTER * 32, :] = quarter


def straight_kernel(place_ref, filters_ref, out_ref):
    lanes = pl.ds(pl.multiple_of(place_ref[2] * 128, 128), 128)
    half = filters_ref[0:STRAIGHT, :, lanes].reshape(STRAIGHT * 32, 128)
    for c in range(8):
        out_ref[c] = half


def neighbours(value):
    z = lax.broadcasted_iota(jnp.int32, value.shape, 1)
    before = jnp.where(z == 0, 0.0, pltpu.roll(value, 1, 1))
    after = jnp.where(z == NZ - 1, 0.0, pltpu.roll(value, NZ - 1, 1))
    return before.astype(BF), after.astype(BF)


def unpack_kernel(place_ref, near_ref, low_ref, high_ref, v3_ref):
    core = place_ref[2]
    row = lax.broadcasted_iota(jnp.int32, (1024, C), 0)
    col = lax.broadcasted_iota(jnp.int32, (1024, C), 1) ^ (core * 128)
    same = ((row >> 7) == (col >> 5)) & ((row & 31) == (col & 31))
    for j in range(4):
        sel = (same & (((row >> 5) & 3) == j)).astype(F32).astype(BF)
        for b in range(4):
            y = b * 4 + j - 1
            if y < 0 or y >= 14:
                continue
            src = (low_ref, near_ref, near_ref, high_ref)[b]
            at = 176 if b == 2 else 0
            rows = jnp.concatenate([src[c, at : at + 176, :] for c in range(8)], axis=1)
            value = dot_n(rows, sel).reshape(22, NZ, C)
            before, after = neighbours(value)
            v3_ref[:, y * 8 : y * 8 + 8, 0:C] = before
            v3_ref[:, y * 8 : y * 8 + 8, C : 2 * C] = value.astype(BF)
            v3_ref[:, y * 8 : y * 8 + 8, 2 * C : 3 * C] = after


def turn_kernel(place_ref, near_ref, q1_ref, q2_ref, q3_ref, straight_ref, out_ref):
    def turn(t, carry):
        at = pl.ds(pl.multiple_of(t * 32, 32), 32)
        rows = jnp.concatenate([straight_ref[c, at, :] for c in range(8)], axis=0)
        out_ref[t] = rows.T
        return carry

    lax.fori_loop(0, STRAIGHT, turn, 0)
    for d, ref in enumerate((near_ref, q1_ref, q2_ref, q3_ref)):
        first = STRAIGHT + QUARTER * lax.rem(place_ref[3] - d + 4, 4)
        for k in range(QUARTER):
            at = k * 32 + (VOL if d == 0 else 0)
            rows = jnp.concatenate([ref[c, at : at + 32, :] for c in range(8)], axis=0)
            out_ref[first + k] = rows.T


def layers_kernel(
    place_ref, v3_ref, mine_ref, other_ref, w2_ref,
    grad_ref, gxl_ref, gxh_ref, gyl_ref, gyh_ref,
    keep_ref, send_ref, d3_ref,
    a3_ref, acc_ref, og_ref, dt_ref, g_ref,
):
    chan, space, core = place_ref[0], place_ref[1], place_ref[2]

    def first(i, carry):
        x0 = i * 5
        for s in range(9):
            part = v3_ref[pl.ds(x0 + s // 3, 5), (s % 3) * 8 : (s % 3) * 8 + 96, :]
            w = [h[3 * s + k] for k in range(3) for h in (mine_ref, other_ref)]
            part = dot_n(part.reshape(480, 3 * C), jnp.concatenate(w, axis=0))
            if s == 0:
                acc_ref[...] = part
            else:
                acc_ref[...] += part
        v = acc_ref[...]
        act = (v / (1.0 + jnp.exp(-v))).astype(BF)
        wide = act.astype(F32).reshape(60, NZ, C)
        before, after = neighbours(wide)
        a3_ref[pl.ds(x0, 5), :, 0:C] = before.reshape(5, 96, C)
        a3_ref[pl.ds(x0, 5), :, C : 2 * C] = act.reshape(5, 96, C)
        a3_ref[pl.ds(x0, 5), :, 2 * C : 3 * C] = after.reshape(5, 96, C)
        return carry

    lax.fori_loop(0, 4, first, 0)

    @pl.when(chan == 0)
    def _():
        a3_ref[0:2] = jnp.zeros((2, 96, 3 * C), BF)

    @pl.when(chan == 7)
    def _():
        a3_ref[18:20] = jnp.zeros((2, 96, 3 * C), BF)

    @pl.when(space == 0)
    def _():
        a3_ref[:, 0:16, :] = jnp.zeros((20, 16, 3 * C), BF)

    @pl.when(space == 15)
    def _():
        a3_ref[:, 80:96, :] = jnp.zeros((20, 16, 3 * C), BF)

    og_ref[1:17, 8:72, :] = grad_ref[...]
    og_ref[0:1, 8:72, :] = gxl_ref[...]
    og_ref[17:18, 8:72, :] = gxh_ref[...]
    og_ref[:, 0:8, :] = gyl_ref[...]
    og_ref[:, 72:80, :] = gyh_ref[...]

    def second(i, carry):
        x0 = i * 6
        for s in range(9):
            part = a3_ref[pl.ds(x0 + s // 3, 6), (s % 3) * 8 : (s % 3) * 8 + 80, :]
            part = dot_n(part.reshape(480, 3 * C), w2_ref[s])
            if s == 0:
                acc_ref[...] = part
            else:
                acc_ref[...] += part
        v = acc_ref[...]
        sig = 1.0 / (1.0 + jnp.exp(-v))
        og = og_ref[pl.ds(x0, 6)].reshape(480, C).astype(F32)
        delta = (og * sig * (1.0 + v * (1.0 - sig))).astype(BF)
        before, after = neighbours(delta.astype(F32).reshape(60, NZ, C))
        d3_ref[pl.ds(x0, 6), :, 0:C] = after.reshape(6, 80, C)
        d3_ref[pl.ds(x0, 6), :, C : 2 * C] = delta.reshape(6, 80, C)
        d3_ref[pl.ds(x0, 6), :, 2 * C : 3 * C] = before.reshape(6, 80, C)
        return carry

    lax.fori_loop(0, 3, second, 0)

    dt_ref[...] = d3_ref[1:17, 8:72, C : 2 * C].reshape(1024, C).T
    for s in range(9):
        part = a3_ref[1 + s // 3 : 17 + s // 3, (1 + s % 3) * 8 : (1 + s % 3) * 8 + 64, :]
        g = dot_n(dt_ref[...], part.reshape(1024, 3 * C)).astype(BF)
        for tz in range(3):
            t = 3 * s + tz
            g_ref[t * C : (t + 1) * C, :] = g[:, tz * C : (tz + 1) * C]
    g_ref[27 * C : 28 * C, :] = jnp.zeros((C, C), BF)
    keep_ref[...] = g_ref[pl.ds(pl.multiple_of(core * SLOT, 16), SLOT), :]
    send_ref[...] = g_ref[pl.ds(pl.multiple_of((1 - core) * SLOT, 16), SLOT), :]


def flip_kernel(w_ref, out_ref):
    def turn(s, carry):
        for k in range(3):
            out_ref[s, k * C : (k + 1) * C, :] = w_ref[s, k * C : (k + 1) * C, :].T
        return carry

    lax.fori_loop(0, 9, turn, 0)


def back_kernel(d3_ref, w2_ref, out_ref, acc_ref):
    for s in range(9):
        tx, ty = s // 3, s % 3
        part = d3_ref[2 - tx : 18 - tx, (2 - ty) * 8 : (2 - ty) * 8 + 64, :]
        part = dot_n(part.reshape(1024, 3 * C), w2_ref[s])
        if s == 0:
            acc_ref[...] = part
        elif s < 8:
            acc_ref[...] += part
        else:
            out_ref[...] = (acc_ref[...] + part).astype(BF).reshape(BX, 64, C)


def finish_kernel(own, place_ref, sums_ref, *refs):
    out_ref, tile_ref, sems = refs[-3:]
    half = place_ref[2] if own else 1 - place_ref[2]
    count = TAPS - half

    def copy(t):
        return pltpu.make_async_copy(
            tile_ref.at[t], out_ref.at[half * TAPS + t], sems.at[t]
        )

    def turn(t, carry):
        at = pl.multiple_of(t * C, C)
        tile_ref[t] = sums_ref[pl.ds(at, C), :].T.astype(F32)
        copy(t).start()
        return carry

    def wait(t, carry):
        copy(t).wait()
        return carry

    lax.fori_loop(0, count, turn, 0)
    lax.fori_loop(0, count, wait, 0)


def border(count):
    up = [(i, i + 1) for i in range(count - 1)]
    return up, [(b, a) for a, b in up]


def local(volume, first_filters, second_filters, out_grad):
    chan, slab, core = (lax.axis_index(a) for a in ("chan", "slab", "core"))
    along_y = lax.rem(slab, 4)
    place = jnp.stack([chan, slab * 2 + core, core, along_y]).astype(jnp.int32)
    swap = [(0, 1), (1, 0)]
    up, down = border(16)
    xup, xdown = border(8)
    space = ("slab", "core")

    og = out_grad.reshape(BX, BY * NZ, C)
    gxl = lax.ppermute(og[BX - 1 :], "chan", xup)
    gxh = lax.ppermute(og[:1], "chan", xdown)

    w1 = jnp.transpose(first_filters, (0, 1, 2, 4, 3)).reshape(27, 32, C)
    packed = pl.pallas_call(
        pack_kernel,
        out_shape=jax.ShapeDtypeStruct((8, VOL + QUARTER * 32, 128), BF),
        in_specs=[SMEM, VMEM, VMEM],
        out_specs=VMEM,
        scratch_shapes=[pltpu.VMEM((2, 8 * 176, 128), F32)],
        compiler_params=params(16),
        cost_estimate=cost(16 * 176 * 128 * 256, 3 << 20),
        name="pack",
    )(place, jnp.transpose(volume, (1, 2, 3, 0)), w1)
    straight = pl.pallas_call(
        straight_kernel,
        out_shape=jax.ShapeDtypeStruct((8, STRAIGHT * 32, 128), BF),
        in_specs=[SMEM, VMEM],
        out_specs=VMEM,
        compiler_params=params(8),
        cost_estimate=cost(1e6, 2 << 20),
        name="straight",
    )(place, w1)
    near = lax.all_to_all(packed, "chan", 0, 0, tiled=True)

    w2 = second_filters.reshape(9, 3 * C, C)
    w2_back = pl.pallas_call(
        flip_kernel,
        out_shape=jax.ShapeDtypeStruct((9, 3 * C, C), BF),
        in_specs=[VMEM],
        out_specs=VMEM,
        compiler_params=params(12),
        cost_estimate=cost(1e9, 7 << 20),
        name="flip",
    )(w2)
    near, gxl, gxh, straight, w2_back = lax.optimization_barrier(
        (near, gxl, gxh, straight, w2_back)
    )
    straight = lax.all_to_all(straight, "chan", 0, 0, tiled=True)
    quarters = [
        lax.ppermute(
            near[:, VOL:],
            "slab",
            [(z + y, z + (y + d) % 4) for z in (0, 4) for y in range(4)],
        )
        for d in range(1, 4)
    ]

    low = lax.ppermute(near[:, 176:VOL], space, up)
    high = lax.ppermute(near[:, :176], space, down)
    low, high, gxl, gxh = lax.optimization_barrier((low, high, gxl, gxh))

    top = jnp.concatenate([gxl[:, 56:], og[:, 56:], gxh[:, 56:]], axis=0)
    bottom = jnp.concatenate([gxl[:, :8], og[:, :8], gxh[:, :8]], axis=0)
    gyl = lax.ppermute(top, space, up)
    gyh = lax.ppermute(bottom, space, down)
    gyl, gyh, low, high, straight = lax.optimization_barrier((gyl, gyh, low, high, straight))
    v3 = pl.pallas_call(
        unpack_kernel,
        out_shape=jax.ShapeDtypeStruct((22, 112, 3 * C), BF),
        in_specs=[SMEM, VMEM, VMEM, VMEM],
        out_specs=VMEM,
        compiler_params=params(16),
        cost_estimate=cost(1.5e9, 6 << 20),
        name="unpack",
    )(place, near, low, high)

    mine = pl.pallas_call(
        turn_kernel,
        out_shape=jax.ShapeDtypeStruct((27, 128, C), BF),
        in_specs=[SMEM] + [VMEM] * 5,
        out_specs=VMEM,
        compiler_params=params(12),
        cost_estimate=cost(1e9, 4 << 20),
        name="turn",
    )(place, near, *quarters, straight)
    other = lax.ppermute(mine, "core", swap)

    keep, send, d3 = pl.pallas_call(
        layers_kernel,
        out_shape=(
            jax.ShapeDtypeStruct((SLOT, C), BF),
            jax.ShapeDtypeStruct((SLOT, C), BF),
            jax.ShapeDtypeStruct((18, 80, 3 * C), BF),
        ),
        in_specs=[SMEM] + [VMEM] * 9,
        out_specs=(VMEM, VMEM, VMEM),
        scratch_shapes=[
            pltpu.VMEM((20, 96, 3 * C), BF),
            pltpu.VMEM((480, C), F32),
            pltpu.VMEM((18, 80, C), BF),
            pltpu.VMEM((C, 1024), BF),
            pltpu.VMEM((2 * SLOT, C), BF),
        ],
        compiler_params=params(30),
        cost_estimate=cost(16e9, 20 << 20),
        name="layers",
    )(place, v3, mine, other, w2, og, gxl, gxh, gyl, gyh)

    received = lax.ppermute(send, "core", swap)
    act_grad = pl.pallas_call(
        back_kernel,
        out_shape=jax.ShapeDtypeStruct((BX, BY * NZ, C), BF),
        in_specs=[VMEM, VMEM],
        out_specs=VMEM,
        scratch_shapes=[pltpu.VMEM((1024, C), F32)],
        compiler_params=params(16),
        cost_estimate=cost(3.6e9, 7 << 20),
        name="back",
    )(d3, w2_back)

    received, act_grad = lax.optimization_barrier((received, act_grad))
    both = (keep.astype(F32) + received.astype(F32)).astype(BF).reshape(64, 56, C)
    shares = lax.all_to_all(both, CHIPS, 0, 0, tiled=True)
    scale = 1.0 / math.sqrt(128 * 128 * NZ)
    share = (jnp.sum(shares.astype(F32), axis=0) * scale).astype(BF)
    spread = lax.optimization_barrier(jnp.broadcast_to(share[None], (64, 56, C)))
    ours = lax.all_to_all(spread, CHIPS, 0, 0, tiled=True).reshape(SLOT, C)
    theirs = lax.ppermute(ours, "core", swap)
    anywhere = pl.BlockSpec(memory_space=pl.ANY)

    def finish(own, *operands):
        return pl.pallas_call(
            functools.partial(finish_kernel, own),
            out_shape=jax.ShapeDtypeStruct((27, C, C), F32),
            in_specs=[SMEM, VMEM] + [anywhere] * (len(operands) - 2),
            out_specs=anywhere,
            scratch_shapes=[pltpu.VMEM((TAPS, C, C), F32), pltpu.SemaphoreType.DMA((TAPS,))],
            input_output_aliases={2: 0} if len(operands) > 2 else {},
            compiler_params=params(12),
            cost_estimate=cost(1e9, 5 << 20),
            name="finish",
        )(*operands)

    filter_grad = finish(True, place, ours)
    filter_grad = finish(False, place, theirs, filter_grad)
    return (
        act_grad.reshape(BX, BY, NZ, C),
        filter_grad.reshape(3, 3, 3, C, C),
    )


def solution(mesh):
    cells = Mesh(mesh.devices.reshape(8, 8, 2), ("chan", "slab", "core"))
    space = ("slab", "core")
    placed = (
        P(None, space, None, "chan"),
        P(None, None, None, None, "chan"),
        P(),
        P("chan", space, None, None),
    )
    return jax.shard_map(
        local,
        mesh=cells,
        in_specs=placed,
        out_specs=(P("chan", space, None, None), P()),
        check_vma=False,
    )
```

```python
import functools
import math

import jax
import jax.numpy as jnp
from jax import lax
from jax.experimental import pallas as pl
from jax.experimental.pallas import tpu as pltpu
from jax.sharding import Mesh
from jax.sharding import PartitionSpec as P

BF = jnp.bfloat16
F32 = jnp.float32
C = 256
NZ = 8
BX, BY = 16, 8
TAPS = 14
SLOT = TAPS * C
VOL = 352
STRAIGHT = 15
QUARTER = (27 - STRAIGHT) // 4
CHIPS = ("chan", "slab")
VMEM = pl.BlockSpec(memory_space=pltpu.VMEM)
SMEM = pl.BlockSpec(memory_space=pltpu.SMEM)


def params(mib):
    return pltpu.CompilerParams(vmem_limit_bytes=mib << 20)


def cost(flops, moved):
    return pl.CostEstimate(flops=int(flops), bytes_accessed=int(moved), transcendentals=0)


def dot_t(a, b):
    return lax.dot_general(a, b, (((1,), (1,)), ((), ())), preferred_element_type=F32)


def dot_n(a, b):
    return lax.dot_general(a, b, (((1,), (0,)), ((), ())), preferred_element_type=F32)


def pack_kernel(place_ref, vol_ref, filters_ref, out_ref, straight_ref, wide_ref):
    row = lax.broadcasted_iota(jnp.int32, (176, 128), 0)
    col = lax.broadcasted_iota(jnp.int32, (176, 128), 1)
    c = sum((row >= 22 * n).astype(jnp.int32) for n in range(1, 8))
    pick = (col == row - 6 * c - 3).astype(F32).astype(BF)
    for quad in range(2):
        for z in range(NZ):
            rows = jnp.concatenate([vol_ref[quad * 4 + j, z] for j in range(4)], axis=0)
            wide_ref[quad, pl.ds(z, 176, stride=8), :] = dot_t(pick, rows)
    lanes = pl.ds(pl.multiple_of(place_ref[2] * 128, 128), 128)
    mine = pl.ds(STRAIGHT + QUARTER * place_ref[3], QUARTER)
    quarter = filters_ref[mine, :, lanes].reshape(QUARTER * 32, 128)
    straight = filters_ref[0:STRAIGHT, :, lanes].reshape(STRAIGHT * 32, 128)
    for c in range(8):
        for quad in range(2):
            part = wide_ref[quad, c * 176 : c * 176 + 176, :]
            out_ref[c, quad * 176 : quad * 176 + 176, :] = part.astype(BF)
        out_ref[c, VOL : VOL + QUARTER * 32, :] = quarter
        straight_ref[c] = straight


def neighbours(value):
    z = lax.broadcasted_iota(jnp.int32, value.shape, 1)
    before = jnp.where(z == 0, 0.0, pltpu.roll(value, 1, 1))
    after = jnp.where(z == NZ - 1, 0.0, pltpu.roll(value, NZ - 1, 1))
    return before.astype(BF), after.astype(BF)


def unpack_kernel(place_ref, near_ref, low_ref, high_ref, v3_ref):
    core = place_ref[2]
    row = lax.broadcasted_iota(jnp.int32, (1024, C), 0)
    col = lax.broadcasted_iota(jnp.int32, (1024, C), 1) ^ (core * 128)
    same = ((row >> 7) == (col >> 5)) & ((row & 31) == (col & 31))
    for j in range(4):
        sel = (same & (((row >> 5) & 3) == j)).astype(F32).astype(BF)
        for b in range(4):
            y = b * 4 + j - 1
            if y < 0 or y >= 14:
                continue
            src = (low_ref, near_ref, near_ref, high_ref)[b]
            at = 176 if b == 2 else 0
            rows = jnp.concatenate([src[c, at : at + 176, :] for c in range(8)], axis=1)
            value = dot_n(rows, sel).reshape(22, NZ, C)
            before, after = neighbours(value)
            v3_ref[:, y * 8 : y * 8 + 8, 0:C] = before
            v3_ref[:, y * 8 : y * 8 + 8, C : 2 * C] = value.astype(BF)
            v3_ref[:, y * 8 : y * 8 + 8, 2 * C : 3 * C] = after


def turn_kernel(place_ref, near_ref, q1_ref, q2_ref, q3_ref, straight_ref, out_ref):
    def turn(t, carry):
        at = pl.ds(pl.multiple_of(t * 32, 32), 32)
        rows = jnp.concatenate([straight_ref[c, at, :] for c in range(8)], axis=0)
        out_ref[t] = rows.T
        return carry

    lax.fori_loop(0, STRAIGHT, turn, 0)
    for d, ref in enumerate((near_ref, q1_ref, q2_ref, q3_ref)):
        first = STRAIGHT + QUARTER * lax.rem(place_ref[3] - d + 4, 4)
        for k in range(QUARTER):
            at = k * 32 + (VOL if d == 0 else 0)
            rows = jnp.concatenate([ref[c, at : at + 32, :] for c in range(8)], axis=0)
            out_ref[first + k] = rows.T


def layers_kernel(
    place_ref, v3_ref, mine_ref, other_ref, w2_ref,
    grad_ref, gxl_ref, gxh_ref, gyl_ref, gyh_ref,
    keep_ref, send_ref, d3_ref,
    a3_ref, acc_ref, og_ref, dt_ref, g_ref,
):
    chan, space, core = place_ref[0], place_ref[1], place_ref[2]

    def first(i, carry):
        x0 = i * 10
        for s in range(9):
            part = v3_ref[pl.ds(x0 + s // 3, 10), (s % 3) * 8 : (s % 3) * 8 + 96, :]
            w = [h[3 * s + k] for k in range(3) for h in (mine_ref, other_ref)]
            part = dot_n(part.reshape(960, 3 * C), jnp.concatenate(w, axis=0))
            if s == 0:
                acc_ref[...] = part
            else:
                acc_ref[...] += part
        v = acc_ref[...]
        act = (v / (1.0 + jnp.exp(-v))).astype(BF)
        wide = act.astype(F32).reshape(120, NZ, C)
        before, after = neighbours(wide)
        a3_ref[pl.ds(x0, 10), :, 0:C] = before.reshape(10, 96, C)
        a3_ref[pl.ds(x0, 10), :, C : 2 * C] = act.reshape(10, 96, C)
        a3_ref[pl.ds(x0, 10), :, 2 * C : 3 * C] = after.reshape(10, 96, C)
        return carry

    lax.fori_loop(0, 2, first, 0)

    @pl.when(chan == 0)
    def _():
        a3_ref[0:2] = jnp.zeros((2, 96, 3 * C), BF)

    @pl.when(chan == 7)
    def _():
        a3_ref[18:20] = jnp.zeros((2, 96, 3 * C), BF)

    @pl.when(space == 0)
    def _():
        a3_ref[:, 0:16, :] = jnp.zeros((20, 16, 3 * C), BF)

    @pl.when(space == 15)
    def _():
        a3_ref[:, 80:96, :] = jnp.zeros((20, 16, 3 * C), BF)

    og_ref[1:17, 8:72, :] = grad_ref[...]
    og_ref[0:1, 8:72, :] = gxl_ref[...]
    og_ref[17:18, 8:72, :] = gxh_ref[...]
    og_ref[:, 0:8, :] = gyl_ref[...]
    og_ref[:, 72:80, :] = gyh_ref[...]

    def second(i, carry):
        x0 = i * 9
        for s in range(9):
            part = a3_ref[pl.ds(x0 + s // 3, 9), (s % 3) * 8 : (s % 3) * 8 + 80, :]
            part = dot_n(part.reshape(720, 3 * C), w2_ref[s])
            if s == 0:
                acc_ref[0:720] = part
            else:
                acc_ref[0:720] += part
        v = acc_ref[0:720]
        sig = 1.0 / (1.0 + jnp.exp(-v))
        og = og_ref[pl.ds(x0, 9)].reshape(720, C).astype(F32)
        delta = (og * sig * (1.0 + v * (1.0 - sig))).astype(BF)
        before, after = neighbours(delta.astype(F32).reshape(90, NZ, C))
        d3_ref[pl.ds(x0, 9), :, 0:C] = after.reshape(9, 80, C)
        d3_ref[pl.ds(x0, 9), :, C : 2 * C] = delta.reshape(9, 80, C)
        d3_ref[pl.ds(x0, 9), :, 2 * C : 3 * C] = before.reshape(9, 80, C)
        return carry

    lax.fori_loop(0, 2, second, 0)

    dt_ref[...] = d3_ref[1:17, 8:72, C : 2 * C].reshape(1024, C).T
    for s in range(9):
        part = a3_ref[1 + s // 3 : 17 + s // 3, (1 + s % 3) * 8 : (1 + s % 3) * 8 + 64, :]
        g = dot_n(dt_ref[...], part.reshape(1024, 3 * C)).astype(BF)
        for tz in range(3):
            t = 3 * s + tz
            g_ref[t * C : (t + 1) * C, :] = g[:, tz * C : (tz + 1) * C]
    g_ref[27 * C : 28 * C, :] = jnp.zeros((C, C), BF)
    keep_ref[...] = g_ref[pl.ds(pl.multiple_of(core * SLOT, 16), SLOT), :]
    send_ref[...] = g_ref[pl.ds(pl.multiple_of((1 - core) * SLOT, 16), SLOT), :]


def flip_kernel(w_ref, out_ref):
    def turn(s, carry):
        for k in range(3):
            out_ref[s, k * C : (k + 1) * C, :] = w_ref[s, k * C : (k + 1) * C, :].T
        return carry

    lax.fori_loop(0, 9, turn, 0)


def back_kernel(d3_ref, w2_ref, out_ref, acc_ref):
    for s in range(9):
        tx, ty = s // 3, s % 3
        part = d3_ref[2 - tx : 18 - tx, (2 - ty) * 8 : (2 - ty) * 8 + 64, :]
        part = dot_n(part.reshape(1024, 3 * C), w2_ref[s])
        if s == 0:
            acc_ref[...] = part
        elif s < 8:
            acc_ref[...] += part
        else:
            out_ref[...] = (acc_ref[...] + part).astype(BF).reshape(BX, 64, C)


def finish_kernel(own, place_ref, sums_ref, *refs):
    out_ref, tile_ref, sems = refs[-3:]
    half = place_ref[2] if own else 1 - place_ref[2]
    count = TAPS - half

    def copy(t):
        return pltpu.make_async_copy(
            tile_ref.at[t], out_ref.at[half * TAPS + t], sems.at[t]
        )

    def turn(t, carry):
        at = pl.multiple_of(t * C, C)
        tile_ref[t] = sums_ref[pl.ds(at, C), :].T.astype(F32)
        copy(t).start()
        return carry

    def wait(t, carry):
        copy(t).wait()
        return carry

    lax.fori_loop(0, count, turn, 0)
    lax.fori_loop(0, count, wait, 0)


def border(count):
    up = [(i, i + 1) for i in range(count - 1)]
    return up, [(b, a) for a, b in up]


def local(volume, first_filters, second_filters, out_grad):
    chan, slab, core = (lax.axis_index(a) for a in ("chan", "slab", "core"))
    along_y = lax.rem(slab, 4)
    place = jnp.stack([chan, slab * 2 + core, core, along_y]).astype(jnp.int32)
    swap = [(0, 1), (1, 0)]
    up, down = border(16)
    xup, xdown = border(8)
    space = ("slab", "core")

    og = out_grad.reshape(BX, BY * NZ, C)
    gxl = lax.ppermute(og[BX - 1 :], "chan", xup)
    gxh = lax.ppermute(og[:1], "chan", xdown)

    packed, straight = pl.pallas_call(
        pack_kernel,
        out_shape=(
            jax.ShapeDtypeStruct((8, VOL + QUARTER * 32, 128), BF),
            jax.ShapeDtypeStruct((8, STRAIGHT * 32, 128), BF),
        ),
        in_specs=[SMEM, VMEM, VMEM],
        out_specs=(VMEM, VMEM),
        scratch_shapes=[pltpu.VMEM((2, 8 * 176, 128), F32)],
        compiler_params=params(16),
        cost_estimate=cost(16 * 176 * 128 * 256, 3 << 20),
        name="pack",
    )(
        place,
        jnp.transpose(volume, (1, 2, 3, 0)),
        jnp.transpose(first_filters, (0, 1, 2, 4, 3)).reshape(27, 32, C),
    )
    near = lax.all_to_all(packed, "chan", 0, 0, tiled=True)

    w2 = second_filters.reshape(9, 3 * C, C)
    w2_back = pl.pallas_call(
        flip_kernel,
        out_shape=jax.ShapeDtypeStruct((9, 3 * C, C), BF),
        in_specs=[VMEM],
        out_specs=VMEM,
        compiler_params=params(12),
        cost_estimate=cost(1e9, 7 << 20),
        name="flip",
    )(w2)
    near, gxl, gxh, straight, w2_back = lax.optimization_barrier(
        (near, gxl, gxh, straight, w2_back)
    )
    straight = lax.all_to_all(straight, "chan", 0, 0, tiled=True)
    quarters = [
        lax.ppermute(
            near[:, VOL:],
            "slab",
            [(z + y, z + (y + d) % 4) for z in (0, 4) for y in range(4)],
        )
        for d in range(1, 4)
    ]

    low = lax.ppermute(near[:, 176:VOL], space, up)
    high = lax.ppermute(near[:, :176], space, down)
    low, high, gxl, gxh = lax.optimization_barrier((low, high, gxl, gxh))

    top = jnp.concatenate([gxl[:, 56:], og[:, 56:], gxh[:, 56:]], axis=0)
    bottom = jnp.concatenate([gxl[:, :8], og[:, :8], gxh[:, :8]], axis=0)
    gyl = lax.ppermute(top, space, up)
    gyh = lax.ppermute(bottom, space, down)
    gyl, gyh, low, high, straight = lax.optimization_barrier((gyl, gyh, low, high, straight))
    v3 = pl.pallas_call(
        unpack_kernel,
        out_shape=jax.ShapeDtypeStruct((22, 112, 3 * C), BF),
        in_specs=[SMEM, VMEM, VMEM, VMEM],
        out_specs=VMEM,
        compiler_params=params(16),
        cost_estimate=cost(1.5e9, 6 << 20),
        name="unpack",
    )(place, near, low, high)

    mine = pl.pallas_call(
        turn_kernel,
        out_shape=jax.ShapeDtypeStruct((27, 128, C), BF),
        in_specs=[SMEM] + [VMEM] * 5,
        out_specs=VMEM,
        compiler_params=params(12),
        cost_estimate=cost(1e9, 4 << 20),
        name="turn",
    )(place, near, *quarters, straight)
    other = lax.ppermute(mine, "core", swap)

    keep, send, d3 = pl.pallas_call(
        layers_kernel,
        out_shape=(
            jax.ShapeDtypeStruct((SLOT, C), BF),
            jax.ShapeDtypeStruct((SLOT, C), BF),
            jax.ShapeDtypeStruct((18, 80, 3 * C), BF),
        ),
        in_specs=[SMEM] + [VMEM] * 9,
        out_specs=(VMEM, VMEM, VMEM),
        scratch_shapes=[
            pltpu.VMEM((20, 96, 3 * C), BF),
            pltpu.VMEM((960, C), F32),
            pltpu.VMEM((18, 80, C), BF),
            pltpu.VMEM((C, 1024), BF),
            pltpu.VMEM((2 * SLOT, C), BF),
        ],
        compiler_params=params(30),
        cost_estimate=cost(16e9, 20 << 20),
        name="layers",
    )(place, v3, mine, other, w2, og, gxl, gxh, gyl, gyh)

    received = lax.ppermute(send, "core", swap)
    act_grad = pl.pallas_call(
        back_kernel,
        out_shape=jax.ShapeDtypeStruct((BX, BY * NZ, C), BF),
        in_specs=[VMEM, VMEM],
        out_specs=VMEM,
        scratch_shapes=[pltpu.VMEM((1024, C), F32)],
        compiler_params=params(16),
        cost_estimate=cost(3.6e9, 7 << 20),
        name="back",
    )(d3, w2_back)

    received, act_grad = lax.optimization_barrier((received, act_grad))
    both = (keep.astype(F32) + received.astype(F32)).astype(BF).reshape(64, 56, C)
    shares = lax.all_to_all(both, CHIPS, 0, 0, tiled=True)
    scale = 1.0 / math.sqrt(128 * 128 * NZ)
    share = (jnp.sum(shares.astype(F32), axis=0) * scale).astype(BF)
    spread = lax.optimization_barrier(jnp.broadcast_to(share[None], (64, 56, C)))
    ours = lax.all_to_all(spread, CHIPS, 0, 0, tiled=True).reshape(SLOT, C)
    theirs = lax.ppermute(ours, "core", swap)
    anywhere = pl.BlockSpec(memory_space=pl.ANY)

    def finish(own, *operands):
        return pl.pallas_call(
            functools.partial(finish_kernel, own),
            out_shape=jax.ShapeDtypeStruct((27, C, C), F32),
            in_specs=[SMEM, VMEM] + [anywhere] * (len(operands) - 2),
            out_specs=anywhere,
            scratch_shapes=[pltpu.VMEM((TAPS, C, C), F32), pltpu.SemaphoreType.DMA((TAPS,))],
            input_output_aliases={2: 0} if len(operands) > 2 else {},
            compiler_params=params(12),
            cost_estimate=cost(1e9, 5 << 20),
            name="finish",
        )(*operands)

    filter_grad = finish(True, place, ours)
    filter_grad = finish(False, place, theirs, filter_grad)
    return (
        act_grad.reshape(BX, BY, NZ, C),
        filter_grad.reshape(3, 3, 3, C, C),
    )


def solution(mesh):
    cells = Mesh(mesh.devices.reshape(8, 8, 2), ("chan", "slab", "core"))
    space = ("slab", "core")
    placed = (
        P(None, space, None, "chan"),
        P(None, None, None, None, "chan"),
        P(),
        P("chan", space, None, None),
    )
    return jax.shard_map(
        local,
        mesh=cells,
        in_specs=placed,
        out_specs=(P("chan", space, None, None), P()),
        check_vma=False,
    )
```
